32 devices in a mesh: groups: 2 (over x), tm: 8 (over z, y), mp: 2 (over core).
Axes of the slice: x: 2, y: 2, z: 4, core: 2. Of those that a mesh axis runs over, the one named last changes fastest.
Arguments:
- queries: bfloat16 [4096, 512], P(('groups', 'tm'), 'mp'), parts along dimension 0, may hold values from -6 to 6
- keys: bfloat16 [4096, 512], P(('groups', 'tm'), 'mp'), parts along dimension 0, may hold values from -6 to 6
- values: bfloat16 [4096, 512], P(('groups', 'tm'), 'mp'), parts along dimension 0, may hold values from -6 to 6
- residual_in: bfloat16 [4096, 512], P(('groups', 'tm'), 'mp'), parts along dimension 0, may hold values from -6 to 6
- out_proj: bfloat16 [512, 512], P('mp'), may hold values from -0.25 to 0.25
- conv_kernel: bfloat16 [31, 512], P(None, 'mp'), may hold values from -1 to 1
- valid_counts: int32 [16], P('groups'), parts along dimension 0, may hold values from 128 to 256, as said below
- segment_ids: int32 [4096], P('groups'), parts along dimension 0, may hold values from 0 to 3, never falling along the last dimension, each value on 1 to 1024 neighbouring positions
- cotangent: bfloat16 [4096, 512], P(('groups', 'tm'), 'mp'), parts along dimension 0, may hold values from -3 to 3
Outputs:
- output: bfloat16 [4096, 512], P(('groups', 'tm'), 'mp'), parts along dimension 0
- grad_input: bfloat16 [4096, 512], P(('groups', 'tm'), 'mp'), parts along dimension 0
- grad_queries: bfloat16 [4096, 512], P(('groups', 'tm'), 'mp'), parts along dimension 0
- grad_keys: bfloat16 [4096, 512], P(('groups', 'tm'), 'mp'), parts along dimension 0
- grad_values: bfloat16 [4096, 512], P(('groups', 'tm'), 'mp'), parts along dimension 0
The draws below stay inside these ranges and needn't reach their ends.
There are 2 independent parts, one for each index of `groups`. The reference program is written for one: setup_inputs(seed, part) draws one part's arguments, and reference() takes and returns one part's arrays. A program takes and returns all parts, laid end to end along the dimension named above; an argument that names none is the same for every part. Nothing has to cross between parts.
Inputs may be any that keep to these rules, and one draw needn't show every extreme that they name: `valid_counts`: one shard has all 256 frames valid and another only 128. `segment_ids`: ids never fall along the window; each id covers at most 1024 frames and one covers exactly that many.
All inputs are finite; a program needn't handle non-finite values.
Results may differ from the reference program's by a relative error of at most 0.04.
Values may be sent and summed in bfloat16 or wider, within the bound.
A program may use at most 64 MiB of HBM per device.

```python
import math
import jax
import jax.numpy as jnp
import numpy as np
from jax import lax

D = 512
HEADS = 8
HEAD_DIM = 64
KERNEL = 31
SEGMENTS = 4
TOK_DEV = 256
SHARDS = 8
TOKENS = 2048


def draw_queries(key, part):
    drawn = jnp.clip(jax.random.normal(jax.random.fold_in(key, 1), (TOKENS, D), jnp.float32), -6.0, 6.0)
    return drawn.astype(jnp.bfloat16)


def draw_keys(key, part):
    drawn = jnp.clip(jax.random.normal(jax.random.fold_in(key, 2), (TOKENS, D), jnp.float32), -6.0, 6.0)
    return drawn.astype(jnp.bfloat16)


def draw_valid_counts(key, part):
    counts = jax.random.randint(jax.random.fold_in(key, 5), (SHARDS,), TOK_DEV // 2, TOK_DEV + 1)
    full_shard = jax.random.randint(jax.random.fold_in(key, 6), (), 0, SHARDS)
    shard_index = jnp.arange(SHARDS)
    counts = jnp.where(shard_index == full_shard, TOK_DEV, counts)
    counts = jnp.where(shard_index == (full_shard + 1) % SHARDS, TOK_DEV // 2, counts)
    return counts.astype(jnp.int32)


def block_scale(rng, dims, cuts, smallest, high):
    loudness, own = 1.0, jax.random.fold_in(rng, 6)
    for axis_at, blocks in cuts:
        draws = jnp.exp(jax.random.uniform(jax.random.fold_in(own, axis_at), (blocks,), jnp.float32, smallest / len(cuts), high / len(cuts)))
        loudness = loudness * jnp.repeat(draws, dims[axis_at] // blocks).reshape([-1 if axis == axis_at else 1 for axis in range(len(dims))])
    return loudness


def length_profile(amount, total, limit, skew):
    weights = [(1 << 20) // math.isqrt(rank ** skew) + 1 for rank in range(2, amount + 1)]
    rest, given = total - limit - (amount - 1), [1] * (amount - 1)
    while rest > 0:
        candidates = [i for i in range(amount - 1) if given[i] < limit]
        whole, remaining = sum([weights[i] for i in candidates]), rest
        for i in candidates:
            extra = min(limit - given[i], max(1, remaining * weights[i] // whole), rest)
            given[i] = given[i] + extra
            rest = rest - extra
    return np.array([limit] + given)


def uneven(stream_key, count, total, bound, skew):
    if count == 2:
        one = jax.random.randint(stream_key, (), max(1, total - bound), min(bound, total - 1) + 1)
        return jnp.stack([one, total - one])
    tallies = jnp.asarray(length_profile(count, total, bound, skew), jnp.int32)
    pairs = (count - 1) // 2
    donor, receiver = tallies[1:1 + 2 * pairs:2], tallies[2:2 + 2 * pairs:2]
    margin = jnp.minimum(donor - 1, bound - receiver)
    passed = jax.random.randint(jax.random.fold_in(stream_key, 1), (pairs,), 0, 1 << 20) % (margin + 1)
    tallies = tallies.at[1:1 + 2 * pairs:2].set(donor - passed).at[2:2 + 2 * pairs:2].set(receiver + passed)
    return tallies[jax.random.permutation(jax.random.fold_in(stream_key, 2), count)]


def centred(own_key, shape, scale, limit, shards=(), kind=jnp.bfloat16):
    entries = jax.random.normal(own_key, shape, jnp.float32) * scale
    if len(shards) > 0:
        entries = block_scale(own_key, shape, shards, -0.22, 0.18) * entries
    return jnp.clip(entries, min=-limit, max=limit).astype(kind)


def setup_inputs(seed: int = 0, part: int = 0) -> dict:
    arg_keys = jax.random.split(jax.random.key(seed), 10)
    part_splits = jax.random.split(jax.random.fold_in(arg_keys[9], part), 10)
    queries = draw_queries(jax.random.fold_in(jax.random.fold_in(arg_keys[9], part), 71), part)
    keys = draw_keys(jax.random.fold_in(jax.random.fold_in(arg_keys[9], part), 71), part)
    values = centred(part_splits[2], (TOKENS, D), 1.0, 6.0, ((0, 8), (1, 2)))
    residual_in = centred(part_splits[3], (TOKENS, D), 1.0, 6.0, ((0, 8), (1, 2)))
    out_proj = centred(arg_keys[4], (D, D), D ** -0.5, 0.25, ((0, 2),))
    conv_kernel = centred(arg_keys[5], (KERNEL, D), KERNEL ** -0.5, 1.0, ((1, 2),))
    valid_counts = draw_valid_counts(jax.random.fold_in(jax.random.fold_in(arg_keys[9], part), 71), part)
    segment_ids = jnp.searchsorted(jnp.cumsum(uneven(part_splits[7], SEGMENTS, TOKENS, TOKENS // 2, 0)), jnp.arange(TOKENS), side="right").astype(jnp.int32)
    cotangent = centred(part_splits[8], (TOKENS, D), 0.5, 3.0, ((0, 8), (1, 2)))
    return {"queries": queries, "keys": keys, "values": values, "residual_in": residual_in, "out_proj": out_proj, "conv_kernel": conv_kernel, "valid_counts": valid_counts, "segment_ids": segment_ids, "cotangent": cotangent}


MASKED_SCORE = -1e30


def reference(queries, keys, values, residual_in, out_proj, conv_kernel, valid_counts, segment_ids, cotangent):
    window_rows = queries.shape[0]
    score_scale = HEAD_DIM ** -0.5
    positions = jnp.arange(window_rows, dtype=jnp.int32)
    limits = jnp.repeat(valid_counts, TOK_DEV)
    labels = jnp.where((positions % TOK_DEV) < limits, segment_ids, -1)
    earlier = (positions[None, :] < positions[:, None]) & (labels[None, :] == segment_ids[:, None])
    visible = earlier | (positions[None, :] == positions[:, None])

    def split_heads(source):
        return source.reshape(window_rows, HEADS, HEAD_DIM).transpose(1, 0, 2)

    def forward_head(head_args):
        query_head, key_head, value_head = head_args
        scores = jnp.dot(query_head, key_head.T, preferred_element_type=jnp.float32) * score_scale
        masked = jnp.where(visible, scores, MASKED_SCORE)
        row_max = jnp.max(masked, axis=1)
        row_mass = jnp.sum(jnp.where(visible, jnp.exp(scores - row_max[:, None]), 0.0), axis=1)
        log_total = row_max + jnp.log(row_mass)
        weights = jnp.where(visible, jnp.exp(scores - log_total[:, None]), 0.0).astype(jnp.bfloat16)
        head_out = jnp.dot(weights, value_head, preferred_element_type=jnp.float32).astype(jnp.bfloat16)
        return head_out, log_total

    query_heads = split_heads(queries)
    key_heads = split_heads(keys)
    value_heads = split_heads(values)
    heads_out, log_totals = lax.map(forward_head, (query_heads, key_heads, value_heads))
    attention_out = heads_out.transpose(1, 0, 2).reshape(window_rows, D)
    mixed = jnp.dot(attention_out, out_proj, preferred_element_type=jnp.float32)
    hidden = (residual_in.astype(jnp.float32) + mixed).astype(jnp.bfloat16)

    conv_reach = KERNEL - 1
    conv_taps = conv_kernel.astype(jnp.float32)
    extended = jnp.concatenate([jnp.zeros((conv_reach, D), jnp.float32), hidden.astype(jnp.float32)], 0)
    conv_mix = jnp.zeros((window_rows, D), jnp.float32)
    for tap_index in range(KERNEL):
        conv_mix = conv_mix + conv_taps[tap_index] * extended[conv_reach - tap_index:conv_reach - tap_index + window_rows]
    output = (hidden.astype(jnp.float32) + jax.nn.silu(conv_mix)).astype(jnp.bfloat16)

    upstream = cotangent.astype(jnp.float32)
    conv_gate = jax.nn.sigmoid(conv_mix)
    grad_conv = upstream * conv_gate * (1.0 + conv_mix * (1.0 - conv_gate))
    spread = jnp.concatenate([grad_conv, jnp.zeros((conv_reach, D), jnp.float32)], 0)
    grad_hidden = upstream
    for tap_index in range(KERNEL):
        grad_hidden = grad_hidden + conv_taps[tap_index] * spread[tap_index:tap_index + window_rows]
    grad_input = grad_hidden.astype(jnp.bfloat16)
    grad_attention = jnp.dot(grad_input, out_proj.T, preferred_element_type=jnp.float32).astype(jnp.bfloat16)
    grad_heads = split_heads(grad_attention)
    row_dots = jnp.einsum("hqd,hqd->hq", grad_heads.astype(jnp.float32), heads_out.astype(jnp.float32))

    def backward_head(head_args):
        query_head, key_head, value_head, grad_head, total_head, dots_head = head_args
        scores = jnp.dot(query_head, key_head.T, preferred_element_type=jnp.float32) * score_scale
        weights = jnp.where(visible, jnp.exp(scores - total_head[:, None]), 0.0)
        grad_value = jnp.dot(weights.astype(jnp.bfloat16).T, grad_head, preferred_element_type=jnp.float32)
        pushes = jnp.dot(grad_head, value_head.T, preferred_element_type=jnp.float32)
        slopes = (weights * (pushes - dots_head[:, None])).astype(jnp.bfloat16)
        grad_query = jnp.dot(slopes, key_head, preferred_element_type=jnp.float32) * score_scale
        grad_key = jnp.dot(slopes.T, query_head, preferred_element_type=jnp.float32) * score_scale
        return grad_query.astype(jnp.bfloat16), grad_key.astype(jnp.bfloat16), grad_value.astype(jnp.bfloat16)

    grad_q, grad_k, grad_v = lax.map(backward_head, (query_heads, key_heads, value_heads, grad_heads, log_totals, row_dots))

    def merge_heads(source):
        return source.transpose(1, 0, 2).reshape(window_rows, D)

    return output, grad_input, merge_heads(grad_q), merge_heads(grad_k), merge_heads(grad_v)
```

```python
import functools
import math

import jax
import jax.numpy as jnp
from jax import lax
from jax.experimental import pallas as pl
from jax.experimental.pallas import tpu as pltpu
from jax.sharding import PartitionSpec as P

HEAD_DIM = 64
PAIR = 2 * HEAD_DIM
HALO = 32
VMEM_BYTES = 63 * 1024 * 1024
LOG2E = math.log2(math.e)
MASKED = -1e30
MESH = pl.DeviceIdType.MESH
F32, BF16 = jnp.float32, jnp.bfloat16


def dot_nt(a, b):
    return lax.dot_general(a, b, (((1,), (1,)), ((), ())), preferred_element_type=F32)


def dot_nn(a, b):
    return jnp.dot(a, b, preferred_element_type=F32)


class Relay:
    def __init__(self, own, buf, recv, send_z, send_y, s, shards, reach, direction):
        self.own, self.buf, self.recv = own, buf, recv
        self.send_z, self.send_y = send_z, send_y
        self.s, self.shards, self.reach, self.direction = s, shards, reach, direction
        odd = lax.rem(s, 2)
        self.lead = odd == (0 if direction > 0 else 1)
        self.partner = s + 1 - 2 * odd
        self.target = s + 2 * direction
        self.has_target = (s + 2 < shards) if direction > 0 else (s >= 2)

    def exists(self, j):
        return (self.s - j >= 0) if self.direction > 0 else (self.s + j < self.shards)

    def source(self, j):
        return self.own if isinstance(j, int) and j == 0 else self.buf.at[j - 1]

    def z_copy(self, j):
        return pltpu.make_async_remote_copy(
            src_ref=self.source(j), dst_ref=self.buf.at[j + 1],
            send_sem=self.send_z.at[j // 2], recv_sem=self.recv.at[j + 1],
            device_id={"tm": self.target}, device_id_type=MESH)

    def y_copy(self, j, landing):
        return pltpu.make_async_remote_copy(
            src_ref=self.source(j), dst_ref=self.buf.at[landing - 1],
            send_sem=self.send_y.at[j // 2], recv_sem=self.recv.at[landing - 1],
            device_id={"tm": self.partner}, device_id_type=MESH)

    def each(self, j, act, along="zy"):
        at_start = isinstance(j, int) and j == 0
        here = self.exists(j)

        if "z" in along:
            @pl.when(here & self.has_target & (j <= self.reach - 2))
            def _():
                act(self.z_copy(j))

        if "y" not in along:
            return

        @pl.when(here & self.lead & (j <= self.reach - 2))
        def _():
            act(self.y_copy(j, j + 1))

        if not at_start:
            @pl.when(here & jnp.logical_not(self.lead))
            def _():
                act(self.y_copy(j, j - 1))

    def send(self, j, along="zy"):
        self.each(j, lambda copy: copy.start(), along)

    def forward(self, j, along="zy"):
        @pl.when(self.exists(j))
        def _():
            self.wait(j)
            self.send(j, along)

    def finish(self, j):
        self.each(j, lambda copy: copy.wait_send())

    def wait(self, j):
        pltpu.make_async_remote_copy(
            src_ref=self.buf.at[j - 1], dst_ref=self.buf.at[j - 1],
            send_sem=self.send_z.at[0], recv_sem=self.recv.at[j - 1],
            device_id={"tm": self.partner}, device_id_type=MESH).wait_recv()


def kernel(shards, reach, heads,
           counts_ref, seg_in, q_in, k_in, v_in, res_in, w_in, taps_in, cot_in,
           out_ref, gin_ref, gq_ref, gk_ref, gv_ref,
           q_ref, k_ref, v_ref, res_ref, w_ref, taps_ref, cot_ref, seg_ref, load_sem, seg_sem,
           kbuf, vbuf, qbuf, abuf, sbuf, woth, aown, aoth, goth,
           hid, prev, nxt, cnext,
           bias, kept, colown, qm, km, vm, am, otr, stats, atr, dqt, dkacc, dvacc,
           da, ext, shifted, gconv, gown,
           krecv, kz, ky, vrecv, vz, vy, qrecv, qz, qy, arecv, az, ay, srecv, sz, sy,
           pair_send, pair_recv, halo_send, halo_recv):
    rows, width = q_ref.shape
    pairs = width // PAIR
    loads = [pltpu.make_async_copy(src, dst, load_sem.at[index])
             for index, (src, dst) in enumerate((
                 (q_in, q_ref), (k_in, k_ref), (v_in, v_ref), (res_in, res_ref), (w_in, w_ref),
                 (taps_in, taps_ref), (cot_in, cot_ref)))]
    loads += [pltpu.make_async_copy(seg_in.at[pl.ds(shard * rows, rows)], seg_ref.at[shard],
                                    seg_sem.at[shard]) for shard in range(shards)]
    for load in loads:
        load.start()
    s = lax.axis_index("tm")
    mp = lax.axis_index("mp")
    other = 1 - mp
    odd = lax.rem(s, 2)
    scale = HEAD_DIM ** -0.5
    to_log2 = scale * LOG2E

    barrier = pltpu.get_barrier_semaphore()
    for shift in (-2, -1, 1, 2):
        @pl.when((s + shift >= 0) & (s + shift < shards))
        def _():
            pl.semaphore_signal(barrier, inc=1, device_id={"tm": s + shift}, device_id_type=MESH)
    pl.semaphore_signal(barrier, inc=1, device_id={"mp": other}, device_id_type=MESH)
    peers = jnp.minimum(s, 2) + jnp.minimum(shards - 1 - s, 2) + 1
    pl.semaphore_wait(barrier, peers)

    args = (s, shards, reach)

    def part_relays(own, buf, sems, direction):
        return [Relay(own[g], buf.at[g], *(sem.at[g] for sem in sems), *args, direction)
                for g in range(pairs)]

    def col_parts(ref):
        return [ref.at[:, g * PAIR:(g + 1) * PAIR] for g in range(pairs)]

    k_up = part_relays(col_parts(k_in), kbuf, (krecv, kz, ky), 1)
    v_up = part_relays(col_parts(v_in), vbuf, (vrecv, vz, vy), 1)
    q_down = Relay(q_in, qbuf, qrecv, qz, qy, *args, -1)
    a_down = part_relays([da.at[g] for g in range(pairs)], abuf, (arecv, az, ay), -1)
    s_down = Relay(stats, sbuf, srecv, sz, sy, *args, -1)

    for g in range(pairs):
        k_up[g].send(0)
        v_up[g].send(0)
    q_down.send(0)

    def pair_copy(index, src, dst):
        return pltpu.make_async_remote_copy(
            src_ref=src, dst_ref=dst, send_sem=pair_send.at[index], recv_sem=pair_recv.at[index],
            device_id={"mp": other}, device_id_type=MESH)

    own_cols = pl.ds(pl.multiple_of(mp * width, width), width)
    other_cols = pl.ds(pl.multiple_of(other * width, width), width)
    w_copy = pair_copy(0, w_in.at[:, other_cols], woth)
    w_copy.start()

    def halo_copy(index, src, dst, shift):
        return pltpu.make_async_remote_copy(
            src_ref=src, dst_ref=dst, send_sem=halo_send.at[index], recv_sem=halo_recv.at[index],
            device_id={"tm": s + shift}, device_id_type=MESH)

    has_prev, has_next = s > 0, s < shards - 1
    cot_copy = halo_copy(0, cot_in.at[pl.ds(0, HALO)], cnext, -1)
    last_copy = halo_copy(1, hid.at[pl.ds(rows - HALO, HALO)], prev, 1)
    first_copy = halo_copy(2, hid.at[pl.ds(0, HALO)], nxt, -1)

    @pl.when(has_prev)
    def _():
        cot_copy.start()

    @pl.when(jnp.logical_not(has_prev))
    def _():
        prev[...] = jnp.zeros_like(prev)

    @pl.when(jnp.logical_not(has_next))
    def _():
        nxt[...] = jnp.zeros_like(nxt)
        cnext[...] = jnp.zeros_like(cnext)

    for load in loads:
        load.wait()

    lane = lax.broadcasted_iota(jnp.int32, (rows, PAIR), 1)
    low = lane < HEAD_DIM

    def only(block, h):
        keep = low if h % 2 == 0 else jnp.logical_not(low)
        return jnp.where(keep, block.astype(F32), 0.0).astype(BF16)

    def cols(g):
        return slice(g * PAIR, (g + 1) * PAIR)

    def head_rows(h):
        return slice(h * HEAD_DIM, (h + 1) * HEAD_DIM)

    for h in range(heads):
        qm[h] = only(q_ref[:, cols(h // 2)], h)
        km[h] = only(k_ref[:, cols(h // 2)], h)
        vm[h] = only(v_ref[:, cols(h // 2)], h)

    def seg_row(shard):
        return seg_ref[pl.ds(shard, 1), :]

    def label_col(shard):
        position = lax.broadcasted_iota(jnp.int32, (1, rows), 1)
        label = jnp.where(position < counts_ref[shard], seg_row(shard), -1).astype(F32)
        return jnp.broadcast_to(label, (128, rows)).T

    own_seg = seg_row(s).astype(F32)

    def fill_bias(slot, col, segs, diagonal):
        for part in range(rows // 128):
            at = slice(part * 128, (part + 1) * 128)
            seen = col == segs[:, at]
            if diagonal:
                key_at = lax.broadcasted_iota(jnp.int32, (rows, 128), 0)
                query_at = lax.broadcasted_iota(jnp.int32, (rows, 128), 1) + part * 128
                seen = (seen & (key_at < query_at)) | (key_at == query_at)
            bias[slot, :, at] = jnp.where(seen, 0.0, MASKED)

    colown[...] = label_col(s)
    fill_bias(0, colown[...], own_seg, True)

    def forward_pair(slot, g, kblk, vblk, first):
        vtr = vblk.astype(F32).T.astype(BF16)
        for h in (2 * g, 2 * g + 1):
            scores = dot_nt(kblk, qm[h]) * to_log2 + bias[slot]
            kept[slot, h] = scores
            top = jnp.max(scores, axis=0, keepdims=True)
            if not first:
                top = jnp.maximum(stats[h:h + 1, :], top)
            weights = jnp.exp2(scores - top)
            mass = jnp.sum(weights, axis=0, keepdims=True)
            part = dot_nn(vtr[head_rows(h - 2 * g)], weights.astype(BF16))
            if not first:
                fade = jnp.exp2(stats[h:h + 1, :] - top)
                mass = mass + stats[heads + h:heads + h + 1, :] * fade
                part = part + otr[head_rows(h), :] * fade
            stats[h:h + 1, :] = top
            stats[heads + h:heads + h + 1, :] = mass
            otr[head_rows(h), :] = part

    for g in range(pairs):
        forward_pair(0, g, k_ref[:, cols(g)], v_ref[:, cols(g)], True)

    @pl.loop(1, reach + 1)
    def _(i):
        odd_step = lax.rem(i, 2) == 1
        j = jnp.where(odd == 1, i, jnp.where(odd_step, i + 1, i - 1))

        @pl.when(s - j >= 0)
        def _():
            fill_bias(j, label_col(s - j), own_seg, False)

        for g in range(pairs):
            @pl.when(odd_step)
            def _():
                k_up[g].forward(i + 1)
                v_up[g].forward(i + 1)

            @pl.when(s - j >= 0)
            def _():
                @pl.when(lax.rem(j, 2) == 1)
                def _():
                    k_up[g].wait(j)
                    v_up[g].wait(j)

                forward_pair(j, g, kbuf[g, j - 1], vbuf[g, j - 1], False)

        @pl.when(lax.rem(i, 2) == 0)
        def _():
            q_down.forward(i, "z")

    for g in range(pairs):
        for h in (2 * g, 2 * g + 1):
            atr[head_rows(h), :] = otr[head_rows(h), :] / stats[heads + h:heads + h + 1, :]
        block = atr[cols(g), :]
        aown[g] = block.T.astype(BF16)
        atr[cols(g), :] = block.astype(BF16).astype(F32)
        pair_copy(1 + g, aown.at[g], aoth.at[g]).start()
    for h in range(heads):
        stats[h:h + 1, :] = stats[h:h + 1, :] + jnp.log(stats[heads + h:heads + h + 1, :]) * LOG2E

    mixed = res_ref[...].astype(F32)
    w_own = w_ref[:, own_cols]
    for g in range(pairs):
        mixed = mixed + dot_nn(aown[g], w_own[cols(g), :])
    w_copy.wait_recv()
    for g in range(pairs):
        pair_copy(1 + g, aown.at[g], aoth.at[g]).wait_recv()
        mixed = mixed + dot_nn(aoth[g], woth[cols(g), :])
    hid[...] = mixed.astype(BF16)

    @pl.when(has_next)
    def _():
        last_copy.start()

    @pl.when(has_prev)
    def _():
        first_copy.start()

    @pl.loop(1, reach // 2 + 1)
    def _(i):
        q_down.send(2 * i, "y")

    @pl.when(has_next)
    def _():
        first_copy.wait_recv()
        cot_copy.wait_recv()

    @pl.when(has_prev)
    def _():
        last_copy.wait_recv()

    long = rows + HALO
    tap_count = taps_ref.shape[0]
    taps = taps_ref[...].astype(F32)
    ext[0:HALO, :] = prev[...].astype(F32)
    ext[HALO:HALO + rows, :] = hid[...].astype(F32)
    ext[HALO + rows:, :] = nxt[...].astype(F32)
    gconv[long:, :] = jnp.zeros((8, width), F32)
    for r in range(8):
        shifted[r, 8:, :] = ext[8 - r:8 - r + long + HALO - 8, :]
    chunk = 96 if long % 96 == 0 else 32
    for g in range(pairs):
        for start in range(0, long, chunk):
            mix = jnp.zeros((chunk, PAIR), F32)
            for tap in range(tap_count):
                at = HALO + start - 8 * (tap // 8)
                mix = mix + taps[tap:tap + 1, cols(g)] * shifted[tap % 8, at:at + chunk, cols(g)]
            gate = jax.nn.sigmoid(mix)
            for piece in range(start, start + chunk, 32):
                at = slice(piece - start, piece - start + 32)
                if piece < rows:
                    up = cot_ref[piece:piece + 32, cols(g)].astype(F32)
                    hidden = ext[HALO + piece:HALO + piece + 32, cols(g)]
                    out_ref[piece:piece + 32, cols(g)] = (hidden + mix[at] * gate[at]).astype(BF16)
                else:
                    up = cnext[:, cols(g)].astype(F32)
                gconv[piece:piece + 32, cols(g)] = (
                    up * gate[at] * (1.0 + mix[at] * (1.0 - gate[at])))
    for r in range(8):
        shifted[r, 0:long, :] = gconv[r:r + long, :]
    for g in range(pairs):
        for start in range(0, rows, 64):
            grad = cot_ref[start:start + 64, cols(g)].astype(F32)
            for tap in range(tap_count):
                at = start + 8 * (tap // 8)
                grad = grad + taps[tap:tap + 1, cols(g)] * shifted[tap % 8, at:at + 64, cols(g)]
            gown[g, start:start + 64, :] = grad.astype(BF16)
        gin_ref[:, cols(g)] = gown[g]
        pair_copy(1 + pairs + g, gown.at[g], goth.at[g]).start()

    w_mine = [w_ref[:, pl.ds(pl.multiple_of(mp * width + g * PAIR, PAIR), PAIR)] for g in range(pairs)]
    w_far = [w_ref[:, pl.ds(pl.multiple_of(other * width + g * PAIR, PAIR), PAIR)] for g in range(pairs)]
    grad = dot_nt(gown[0], w_mine[0])
    gradt = dot_nt(w_mine[0], gown[0])
    for g in range(1, pairs):
        grad = grad + dot_nt(gown[g], w_mine[g])
        gradt = gradt + dot_nt(w_mine[g], gown[g])
    for g in range(pairs):
        pair_copy(1 + pairs + g, gown.at[g], goth.at[g]).wait_recv()
        grad = grad + dot_nt(goth[g], w_far[g])
        gradt = gradt + dot_nt(w_far[g], goth[g])
    for g in range(pairs):
        da[g] = grad[:, cols(g)].astype(BF16)
    products = gradt.astype(BF16).astype(F32) * atr[...]
    for h in range(heads):
        stats[heads + h:heads + h + 1, :] = jnp.sum(products[head_rows(h)], axis=0, keepdims=True)
    s_down.send(0)
    for g in range(pairs):
        a_down[g].send(0)
    for h in range(heads):
        am[h] = only(da[h // 2], h)

    def query_pair(slot, g, kblk, vblk, first):
        ktr = kblk.astype(F32).T.astype(BF16)
        sums = []
        for h in (2 * g, 2 * g + 1):
            weights = jnp.exp2(kept[slot, h] - stats[h:h + 1, :])
            pushes = dot_nt(vblk, am[h])
            slopes = (weights * (pushes - stats[heads + h:heads + h + 1, :])).astype(BF16)
            part = dot_nn(ktr[head_rows(h - 2 * g)], slopes)
            if first:
                dqt[head_rows(h), :] = part
                sums.append((dot_nn(slopes, q_ref[:, cols(g)]),
                             dot_nn(weights.astype(BF16), da[g])))
            else:
                dqt[head_rows(h), :] = dqt[head_rows(h), :] + part
        if first:
            dkacc[:, cols(g)] = jnp.where(low, sums[0][0], sums[1][0])
            dvacc[:, cols(g)] = jnp.where(low, sums[0][1], sums[1][1])

    for g in range(pairs):
        query_pair(0, g, k_ref[:, cols(g)], v_ref[:, cols(g)], True)

    @pl.loop(1, reach + 1)
    def _(i):
        even_step = lax.rem(i, 2) == 0
        j = jnp.where(odd == 0, i, jnp.where(even_step, i - 1, i + 1))

        @pl.when(s - i >= 0)
        def _():
            for g in range(pairs):
                query_pair(i, g, kbuf[g, i - 1], vbuf[g, i - 1], False)

        @pl.when(jnp.logical_not(even_step))
        def _():
            s_down.forward(i + 1)
            for g in range(pairs):
                a_down[g].forward(i + 1)

        @pl.when(s + j < shards)
        def _():
            fill_bias(reach + 1, colown[...], seg_row(s + j).astype(F32), False)
            odd_slot = lax.rem(j, 2) == 1

            @pl.when(odd_slot)
            def _():
                q_down.wait(j)
                s_down.wait(j)

            for g in range(pairs):
                @pl.when(odd_slot)
                def _():
                    a_down[g].wait(j)

                qblk, ablk, far = qbuf[j - 1, :, cols(g)], abuf[g, j - 1], sbuf[j - 1]
                sums = []
                for h in (2 * g, 2 * g + 1):
                    scores = dot_nt(km[h], qblk) * to_log2 + bias[reach + 1]
                    weights = jnp.exp2(scores - far[h:h + 1, :])
                    pushes = dot_nt(vm[h], ablk)
                    slopes = (weights * (pushes - far[heads + h:heads + h + 1, :])).astype(BF16)
                    sums.append((dot_nn(slopes, qblk), dot_nn(weights.astype(BF16), ablk)))
                dkacc[:, cols(g)] = dkacc[:, cols(g)] + jnp.where(low, sums[0][0], sums[1][0])
                dvacc[:, cols(g)] = dvacc[:, cols(g)] + jnp.where(low, sums[0][1], sums[1][1])

    gq_ref[...] = (dqt[...] * scale).T.astype(BF16)
    gk_ref[...] = (dkacc[...] * scale).astype(BF16)
    gv_ref[...] = dvacc[...].astype(BF16)

    relays = (*k_up, *v_up, q_down, *a_down, s_down)
    for relay in relays:
        relay.finish(0)

    @pl.loop(1, reach // 2 + 1)
    def _(i):
        for relay in relays:
            relay.finish(2 * i)

    w_copy.wait_send()
    for g in range(pairs):
        pair_copy(1 + g, aown.at[g], aoth.at[g]).wait_send()
        pair_copy(1 + pairs + g, gown.at[g], goth.at[g]).wait_send()

    @pl.when(has_prev)
    def _():
        cot_copy.wait_send()
        first_copy.wait_send()

    @pl.when(has_next)
    def _():
        last_copy.wait_send()


def store_kernel(*refs):
    count = len(refs) // 2
    stores = [pltpu.make_async_copy(refs[index], refs[count + index], refs[-1].at[index])
              for index in range(count)]
    for store in stores:
        store.start()
    for store in stores:
        store.wait()


def local(queries, keys, values, residual_in, out_proj, conv_kernel, valid_counts, segment_ids,
          cotangent):
    rows, width = queries.shape
    heads = width // HEAD_DIM
    pairs = width // PAIR
    shards = valid_counts.shape[0]
    window = segment_ids.shape[0]
    reach = -(-(window // 2) // rows)
    block = (rows, width)
    sems = pltpu.SemaphoreType.DMA
    relay_sems = [sems((reach,)), sems((reach // 2 + 1,)), sems((reach // 2 + 1,))]
    part_sems = [sems((pairs,) + each.shape) for each in relay_sems]
    scratch = [pltpu.VMEM(block, BF16)] * 4 + [
        pltpu.VMEM(out_proj.shape, BF16), pltpu.VMEM(conv_kernel.shape, BF16),
        pltpu.VMEM(block, BF16), pltpu.VMEM((shards, rows), jnp.int32),
        pltpu.SemaphoreType.DMA((7,)), pltpu.SemaphoreType.DMA((shards,)),
        pltpu.VMEM((pairs, reach, rows, PAIR), BF16), pltpu.VMEM((pairs, reach, rows, PAIR), BF16),
        pltpu.VMEM((reach,) + block, BF16), pltpu.VMEM((pairs, reach, rows, PAIR), BF16),
        pltpu.VMEM((reach, 2 * heads, rows), F32),
        pltpu.VMEM(block, BF16),
        pltpu.VMEM((pairs, rows, PAIR), BF16), pltpu.VMEM((pairs, rows, PAIR), BF16),
        pltpu.VMEM((pairs, rows, PAIR), BF16),
        pltpu.VMEM(block, BF16), pltpu.VMEM((HALO, width), BF16), pltpu.VMEM((HALO, width), BF16),
        pltpu.VMEM((HALO, width), BF16),
        pltpu.VMEM((reach + 2, rows, rows), F32), pltpu.VMEM((reach + 1, heads, rows, rows), F32), pltpu.VMEM((rows, 128), F32),
        pltpu.VMEM((heads, rows, PAIR), BF16), pltpu.VMEM((heads, rows, PAIR), BF16),
        pltpu.VMEM((heads, rows, PAIR), BF16), pltpu.VMEM((heads, rows, PAIR), BF16),
        pltpu.VMEM((width, rows), F32), pltpu.VMEM((2 * heads, rows), F32),
        pltpu.VMEM((width, rows), F32), pltpu.VMEM((width, rows), F32),
        pltpu.VMEM(block, F32), pltpu.VMEM(block, F32),
        pltpu.VMEM((pairs, rows, PAIR), BF16), pltpu.VMEM((rows + 2 * HALO, width), F32),
        pltpu.VMEM((8, rows + 2 * HALO, width), F32), pltpu.VMEM((rows + HALO + 8, width), F32),
        pltpu.VMEM((pairs, rows, PAIR), BF16),
    ] + part_sems * 2 + relay_sems + part_sems + relay_sems + [
        pltpu.SemaphoreType.DMA((1 + 2 * pairs,)), pltpu.SemaphoreType.DMA((1 + 2 * pairs,)),
        pltpu.SemaphoreType.DMA((3,)), pltpu.SemaphoreType.DMA((3,)),
    ]
    vmem = pl.BlockSpec(memory_space=pltpu.VMEM)
    hbm = pl.BlockSpec(memory_space=pltpu.MemorySpace.HBM)
    results = pl.pallas_call(
        functools.partial(kernel, shards, reach, heads),
        out_shape=(pltpu.VMEM(block, BF16),) * 5,
        in_specs=[pl.BlockSpec(memory_space=pltpu.SMEM)] + [hbm] * 8,
        out_specs=(vmem,) * 5,
        scratch_shapes=scratch,
        compiler_params=pltpu.CompilerParams(
            collective_id=0, has_side_effects=True, vmem_limit_bytes=VMEM_BYTES),
    )(valid_counts, segment_ids, queries, keys, values, residual_in, out_proj,
      conv_kernel, cotangent)
    return pl.pallas_call(
        store_kernel,
        out_shape=(jax.ShapeDtypeStruct(block, BF16),) * 5,
        in_specs=[pl.BlockSpec(memory_space=pl.ANY)] * 5,
        out_specs=(hbm,) * 5,
        scratch_shapes=[pltpu.SemaphoreType.DMA((5,))],
    )(*[pltpu.with_memory_space_constraint(r, pltpu.VMEM) for r in results])


def solution(mesh):
    tokens = P(("groups", "tm"), "mp")
    in_specs = (tokens, tokens, tokens, tokens, P("mp", None), P(None, "mp"), P("groups"),
                P("groups"), tokens)
    return jax.shard_map(local, mesh=mesh, in_specs=in_specs, out_specs=(tokens,) * 5,
                         check_vma=False)
```

```python
import functools
import math

import jax
import jax.numpy as jnp
from jax import lax
from jax.experimental import pallas as pl
from jax.experimental.pallas import tpu as pltpu
from jax.sharding import PartitionSpec as P

HEAD_DIM = 64
PAIR = 2 * HEAD_DIM
HALO = 32
VMEM_BYTES = 63 * 1024 * 1024
LOG2E = math.log2(math.e)
MASKED = -1e30
MESH = pl.DeviceIdType.MESH
F32, BF16 = jnp.float32, jnp.bfloat16


def dot_nt(a, b):
    return lax.dot_general(a, b, (((1,), (1,)), ((), ())), preferred_element_type=F32)


def dot_nn(a, b):
    return jnp.dot(a, b, preferred_element_type=F32)


class Relay:
    def __init__(self, own, slot, recv, send_z, send_y, s, shards, reach, direction):
        self.own, self.slot, self.recv = own, slot, recv
        self.send_z, self.send_y = send_z, send_y
        self.s, self.shards, self.reach, self.direction = s, shards, reach, direction
        odd = lax.rem(s, 2)
        self.lead = odd == (0 if direction > 0 else 1)
        self.partner = s + 1 - 2 * odd
        self.target = s + 2 * direction
        self.has_target = (s + 2 < shards) if direction > 0 else (s >= 2)

    def exists(self, j):
        return (self.s - j >= 0) if self.direction > 0 else (self.s + j < self.shards)

    def source(self, j):
        return self.own if isinstance(j, int) and j == 0 else self.slot(j)

    def z_copy(self, j):
        return pltpu.make_async_remote_copy(
            src_ref=self.source(j), dst_ref=self.slot(j + 2),
            send_sem=self.send_z.at[j // 2], recv_sem=self.recv.at[j + 1],
            device_id={"tm": self.target}, device_id_type=MESH)

    def y_copy(self, j, landing):
        return pltpu.make_async_remote_copy(
            src_ref=self.source(j), dst_ref=self.slot(landing),
            send_sem=self.send_y.at[j // 2], recv_sem=self.recv.at[landing - 1],
            device_id={"tm": self.partner}, device_id_type=MESH)

    def each(self, j, act, along="zy"):
        at_start = isinstance(j, int) and j == 0
        here = self.exists(j)

        if "z" in along:
            @pl.when(here & self.has_target & (j <= self.reach - 2))
            def _():
                act(self.z_copy(j))

        if "y" not in along:
            return

        @pl.when(here & self.lead & (j <= self.reach - 2))
        def _():
            act(self.y_copy(j, j + 1))

        if not at_start:
            @pl.when(here & jnp.logical_not(self.lead))
            def _():
                act(self.y_copy(j, j - 1))

    def send(self, j, along="zy"):
        self.each(j, lambda copy: copy.start(), along)

    def forward(self, j, along="zy"):
        @pl.when(self.exists(j))
        def _():
            self.wait(j)
            self.send(j, along)

    def finish(self, j):
        @pl.when(j <= self.reach)
        def _():
            self.each(j, lambda copy: copy.wait_send())

    def wait(self, j):
        pltpu.make_async_remote_copy(
            src_ref=self.slot(j), dst_ref=self.slot(j),
            send_sem=self.send_z.at[0], recv_sem=self.recv.at[j - 1],
            device_id={"tm": self.partner}, device_id_type=MESH).wait_recv()


def kernel(shards, reach, heads,
           counts_ref, seg_in, q_in, k_in, v_in, res_in, w_in, taps_in, cot_in,
           out_ref, gin_ref, gq_ref, gk_ref, gv_ref,
           q_ref, kv_ref, res_ref, w_ref, taps_ref, cot_ref, seg_ref, load_sem, kv_sem, seg_sem,
           kvbuf, qbuf, abuf, sbuf, woth, aown, aoth, goth,
           hid, prev, nxt, cnext,
           bias, kept, colown, qm, km, vm, am, otr, stats, atr, dqt, dkacc, dvacc,
           da, ext, shifted, spread, gconv, gown,
           qfar, afar, ofar, dfar, part_out, part_stats, far_out, far_stats, part_dq, far_dq,
           kvrecv, kvz, kvy, qrecv, qz, qy, arecv, az, ay, srecv, sz, sy,
           pair_send, pair_recv, halo_send, halo_recv, far_send, far_recv):
    rows, width = q_ref.shape
    pairs = width // PAIR
    kv_loads = [pltpu.make_async_copy(src.at[:, g * PAIR:(g + 1) * PAIR], kv_ref.at[g, index],
                                      kv_sem.at[g, index])
                for g in range(pairs) for index, src in enumerate((k_in, v_in))]
    loads = [pltpu.make_async_copy(src, dst, load_sem.at[index])
             for index, (src, dst) in enumerate((
                 (q_in, q_ref), (res_in, res_ref), (w_in, w_ref),
                 (taps_in, taps_ref), (cot_in, cot_ref)))]
    loads += [pltpu.make_async_copy(seg_in.at[pl.ds(shard * rows, rows)], seg_ref.at[shard],
                                    seg_sem.at[shard]) for shard in range(shards)]
    for load in kv_loads + loads:
        load.start()
    s = lax.axis_index("tm")
    mp = lax.axis_index("mp")
    other = 1 - mp
    odd = lax.rem(s, 2)
    scale = HEAD_DIM ** -0.5
    to_log2 = scale * LOG2E

    barrier = pltpu.get_barrier_semaphore()
    for shift in (-2, -1, 1, 2):
        @pl.when((s + shift >= 0) & (s + shift < shards))
        def _():
            pl.semaphore_signal(barrier, inc=1, device_id={"tm": s + shift}, device_id_type=MESH)
    pl.semaphore_signal(barrier, inc=1, device_id={"mp": other}, device_id_type=MESH)
    peers = jnp.minimum(s, 2) + jnp.minimum(shards - 1 - s, 2) + 1
    pl.semaphore_wait(barrier, peers)

    near = reach - 2

    def part_relays(own, buf, sems, span, direction):
        return [Relay(own.at[g], lambda j, g=g: buf.at[g, j - 1], *(sem.at[g] for sem in sems),
                      s, shards, span, direction) for g in range(pairs)]

    kv_up = part_relays(kv_ref, kvbuf, (kvrecv, kvz, kvy), near, 1)
    q_down = Relay(q_in, lambda j: qbuf.at[j - 1], qrecv, qz, qy, s, shards, reach, -1)
    a_down = part_relays(da, abuf, (arecv, az, ay), reach, -1)
    s_down = Relay(stats, lambda j: sbuf.at[j - 1], srecv, sz, sy, s, shards, reach, -1)

    for load in kv_loads:
        load.wait()
    for g in range(pairs):
        kv_up[g].send(0)
        if g == 0:
            q_down.send(0, "z")

    helps = (s + 2 < shards) & (s >= reach - 3)
    helped = s >= reach - 1

    def far_copy(index, src, dst):
        return pltpu.make_async_remote_copy(
            src_ref=src, dst_ref=dst, send_sem=far_send.at[index], recv_sem=far_recv.at[index],
            device_id={"tm": s + 2}, device_id_type=MESH)

    def far_copies(g):
        return (far_copy(3 * g, part_out.at[g], far_out.at[g]),
                far_copy(3 * g + 1, part_stats.at[g], far_stats.at[g]))

    def far_grad_copy(g):
        return far_copy(3 * g + 2, part_dq.at[g], far_dq.at[g])

    def pair_copy(index, src, dst):
        return pltpu.make_async_remote_copy(
            src_ref=src, dst_ref=dst, send_sem=pair_send.at[index], recv_sem=pair_recv.at[index],
            device_id={"mp": other}, device_id_type=MESH)

    own_cols = pl.ds(pl.multiple_of(mp * width, width), width)
    other_cols = pl.ds(pl.multiple_of(other * width, width), width)
    w_copy = pair_copy(0, w_in.at[:, other_cols], woth)
    w_copy.start()

    def halo_copy(index, src, dst, shift):
        return pltpu.make_async_remote_copy(
            src_ref=src, dst_ref=dst, send_sem=halo_send.at[index], recv_sem=halo_recv.at[index],
            device_id={"tm": s + shift}, device_id_type=MESH)

    has_prev, has_next = s > 0, s < shards - 1
    cot_copy = halo_copy(0, cot_in.at[pl.ds(0, HALO)], cnext, -1)
    last_copy = halo_copy(1, hid.at[pl.ds(rows - HALO, HALO)], prev, 1)
    first_copy = halo_copy(2, hid.at[pl.ds(0, HALO)], nxt, -1)

    @pl.when(has_prev)
    def _():
        cot_copy.start()

    @pl.when(jnp.logical_not(has_prev))
    def _():
        prev[...] = jnp.zeros_like(prev)

    @pl.when(jnp.logical_not(has_next))
    def _():
        nxt[...] = jnp.zeros_like(nxt)
        cnext[...] = jnp.zeros_like(cnext)

    for load in loads:
        load.wait()

    lane = lax.broadcasted_iota(jnp.int32, (rows, PAIR), 1)
    low = lane < HEAD_DIM

    def only(block, h):
        keep = low if h % 2 == 0 else jnp.logical_not(low)
        return jnp.where(keep, block.astype(F32), 0.0).astype(BF16)

    def cols(g):
        return slice(g * PAIR, (g + 1) * PAIR)

    def head_rows(h):
        return slice(h * HEAD_DIM, (h + 1) * HEAD_DIM)

    for h in range(heads):
        qm[h] = only(q_ref[:, cols(h // 2)], h)
        km[h] = only(kv_ref[h // 2, 0], h)
        vm[h] = only(kv_ref[h // 2, 1], h)

    def seg_row(shard):
        return seg_ref[pl.ds(shard, 1), :]

    def label_col(shard):
        position = lax.broadcasted_iota(jnp.int32, (1, rows), 1)
        label = jnp.where(position < counts_ref[shard], seg_row(shard), -1).astype(F32)
        return jnp.broadcast_to(label, (128, rows)).T

    own_seg = seg_row(s).astype(F32)

    def fill_bias(slot, col, segs, diagonal):
        for part in range(rows // 128):
            at = slice(part * 128, (part + 1) * 128)
            seen = col == segs[:, at]
            if diagonal:
                key_at = lax.broadcasted_iota(jnp.int32, (rows, 128), 0)
                query_at = lax.broadcasted_iota(jnp.int32, (rows, 128), 1) + part * 128
                seen = (seen & (key_at < query_at)) | (key_at == query_at)
            bias[slot, :, at] = jnp.where(seen, 0.0, MASKED)

    colown[...] = label_col(s)
    fill_bias(0, colown[...], own_seg, True)

    def forward_pair(g, kblk, vblk, targets):
        vtr = vblk.astype(F32).T.astype(BF16)
        for slot, masked_q, totals, out, first in targets:
            for h in (2 * g, 2 * g + 1):
                at_top, at_mass = totals(h)
                scores = dot_nt(kblk, masked_q[h]) * to_log2 + bias[slot]
                kept[slot, h] = scores
                top = jnp.max(scores, axis=0, keepdims=True)
                if not first:
                    top = jnp.maximum(at_top[...], top)
                weights = jnp.exp2(scores - top)
                mass = jnp.sum(weights, axis=0, keepdims=True)
                part = dot_nn(vtr[head_rows(h - 2 * g)], weights.astype(BF16))
                if not first:
                    fade = jnp.exp2(at_top[...] - top)
                    mass = mass + at_mass[...] * fade
                    part = part + out[head_rows(h), :] * fade
                at_top[...] = top
                at_mass[...] = mass
                out[head_rows(h), :] = part

    def own_totals(h):
        return stats.at[h:h + 1, :], stats.at[heads + h:heads + h + 1, :]

    def far_totals(h):
        g, at = h // 2, h % 2
        return part_stats.at[g, at:at + 1, :], part_stats.at[g, 2 + at:3 + at, :]

    def own_target(slot, first=False):
        return slot, qm, own_totals, otr, first

    def far_target(slot):
        return slot, qfar, far_totals, ofar, False

    for g in range(pairs):
        forward_pair(g, kv_ref[g, 0], kv_ref[g, 1], [own_target(0, True)])
        part_stats[g, 0:2, :] = jnp.full((2, rows), 2 * MASKED, F32)
        part_stats[g, 2:, :] = jnp.zeros((6, rows), F32)
    ofar[...] = jnp.zeros_like(ofar)

    def own_step(i):
        return jnp.where(odd == 1, i, jnp.where(lax.rem(i, 2) == 1, i + 1, i - 1))

    if near > 2:
        @pl.loop(1, near - 1)
        def _(i):
            j = own_step(i)

            @pl.when(s - j >= 0)
            def _():
                fill_bias(j, label_col(s - j), own_seg, False)

            for g in range(pairs):
                @pl.when(lax.rem(i, 2) == 1)
                def _():
                    kv_up[g].forward(i + 1)

                @pl.when(s - j >= 0)
                def _():
                    @pl.when(lax.rem(j, 2) == 1)
                    def _():
                        kv_up[g].wait(j)

                    forward_pair(g, kvbuf[g, j - 1, 0], kvbuf[g, j - 1, 1], [own_target(j)])

    for d in (near - 1, near):
        @pl.when(s - d >= 0)
        def _():
            col = label_col(s - d)
            fill_bias(d, col, own_seg, False)
            fill_bias(d + 2, col, seg_row(jnp.minimum(s + 2, shards - 1)).astype(F32), False)

    q_down.forward(2, "z")
    for j in range(1, reach + 1):
        @pl.when(s + j < shards)
        def _():
            fill_bias(reach + j, colown[...], seg_row(s + j).astype(F32), False)

    for g in range(pairs):
        @pl.when(helps)
        def _():
            for h in (2 * g, 2 * g + 1):
                qfar[h] = only(qbuf[1, :, cols(g)], h)

        kv_up[g].forward(near)
        for step in (near - 1, near):
            j = own_step(step)

            @pl.when(s - j >= 0)
            def _():
                @pl.when(lax.rem(j, 2) == 1)
                def _():
                    kv_up[g].wait(j)

                forward_pair(g, kvbuf[g, j - 1, 0], kvbuf[g, j - 1, 1], [far_target(j + 2), own_target(j)])

        @pl.when(helps)
        def _():
            part_out[g] = ofar[cols(g), :].astype(BF16)
            for copy in far_copies(g):
                copy.start()

    for g in range(pairs):
        @pl.when(helped)
        def _():
            for copy in far_copies(g):
                copy.wait_recv()
            for at in (0, 1):
                h = 2 * g + at
                at_top, at_mass = own_totals(h)
                far_top = far_stats[g, at:at + 1, :]
                top = jnp.maximum(at_top[...], far_top)
                fade, far_fade = jnp.exp2(at_top[...] - top), jnp.exp2(far_top - top)
                at_top[...] = top
                at_mass[...] = at_mass[...] * fade + far_stats[g, 2 + at:3 + at, :] * far_fade
                far_part = far_out[g, head_rows(at), :].astype(F32)
                otr[head_rows(h), :] = otr[head_rows(h), :] * fade + far_part * far_fade

        for h in (2 * g, 2 * g + 1):
            atr[head_rows(h), :] = otr[head_rows(h), :] / stats[heads + h:heads + h + 1, :]
        block = atr[cols(g), :]
        aown[g] = block.T.astype(BF16)
        atr[cols(g), :] = block.astype(BF16).astype(F32)
        pair_copy(1 + g, aown.at[g], aoth.at[g]).start()
    for h in range(heads):
        stats[h:h + 1, :] = stats[h:h + 1, :] + jnp.log(stats[heads + h:heads + h + 1, :]) * LOG2E

    mixed = res_ref[...].astype(F32)
    w_own = w_ref[:, own_cols]
    for g in range(pairs):
        mixed = mixed + dot_nn(aown[g], w_own[cols(g), :])
    w_copy.wait_recv()
    for g in range(pairs):
        pair_copy(1 + g, aown.at[g], aoth.at[g]).wait_recv()
        mixed = mixed + dot_nn(aoth[g], woth[cols(g), :])
    hid[...] = mixed.astype(BF16)

    @pl.when(has_next)
    def _():
        last_copy.start()

    @pl.when(has_prev)
    def _():
        first_copy.start()

    q_down.send(0, "y")
    q_down.send(2, "y")

    @pl.loop(2, reach // 2 + 1)
    def _(i):
        q_down.forward(2 * i)

    long = rows + HALO
    tap_count = taps_ref.shape[0]
    taps = taps_ref[...].astype(F32)

    def shift_hidden(start, stop):
        for r in range(8):
            shifted[r, start:stop, :] = ext[start - r:stop - r, :]

    def shift_grad(start, stop):
        for r in range(8):
            spread[r, start:stop, :] = gconv[start + r:stop + r, :]

    def convolve(g, start, stop):
        size = stop - start
        mix = jnp.zeros((size, PAIR), F32)
        for tap in range(tap_count):
            at = HALO + start - 8 * (tap // 8)
            mix = mix + taps[tap:tap + 1, cols(g)] * shifted[tap % 8, at:at + size, cols(g)]
        gate = jax.nn.sigmoid(mix)
        if start < rows:
            up = cot_ref[start:stop, cols(g)].astype(F32)
            hidden = ext[HALO + start:HALO + stop, cols(g)]
            out_ref[start:stop, cols(g)] = (hidden + mix * gate).astype(BF16)
        else:
            up = cnext[:, cols(g)].astype(F32)
        gconv[start:stop, cols(g)] = up * gate * (1.0 + mix * (1.0 - gate))

    def convolve_back(g, start, stop):
        grad = cot_ref[start:stop, cols(g)].astype(F32)
        for tap in range(tap_count):
            at = start + 8 * (tap // 8)
            grad = grad + taps[tap:tap + 1, cols(g)] * spread[tap % 8, at:at + stop - start, cols(g)]
        gown[g, start:stop, :] = grad.astype(BF16)

    ext[HALO:HALO + rows, :] = hid[...].astype(F32)
    gconv[long:, :] = jnp.zeros((8, width), F32)
    shift_hidden(HALO + 8, HALO + rows)
    step, back_step = (rows - HALO) // 2, (rows - 2 * HALO) // 2
    for g in range(pairs):
        for start in range(HALO, rows, step):
            convolve(g, start, start + step)
    shift_grad(HALO, rows - 8)
    for g in range(pairs):
        for start in range(HALO, rows - HALO, back_step):
            convolve_back(g, start, start + back_step)

    @pl.when(has_next)
    def _():
        first_copy.wait_recv()
        cot_copy.wait_recv()

    @pl.when(has_prev)
    def _():
        last_copy.wait_recv()

    ext[0:HALO, :] = prev[...].astype(F32)
    ext[HALO + rows:, :] = nxt[...].astype(F32)
    shift_hidden(8, HALO + 8)
    shift_hidden(HALO + rows, long + HALO)
    for g in range(pairs):
        convolve(g, 0, HALO)
        convolve(g, rows, long)
    shift_grad(0, HALO)
    shift_grad(rows - 8, long)
    for g in range(pairs):
        convolve_back(g, 0, HALO)
        convolve_back(g, rows - HALO, rows)
        gin_ref[:, cols(g)] = gown[g]
        pair_copy(1 + pairs + g, gown.at[g], goth.at[g]).start()

    w_mine = [w_ref[:, pl.ds(pl.multiple_of(mp * width + g * PAIR, PAIR), PAIR)] for g in range(pairs)]
    w_far = [w_ref[:, pl.ds(pl.multiple_of(other * width + g * PAIR, PAIR), PAIR)] for g in range(pairs)]
    grad = dot_nt(gown[0], w_mine[0])
    gradt = dot_nt(w_mine[0], gown[0])
    for g in range(1, pairs):
        grad = grad + dot_nt(gown[g], w_mine[g])
        gradt = gradt + dot_nt(w_mine[g], gown[g])
    for g in range(pairs):
        pair_copy(1 + pairs + g, gown.at[g], goth.at[g]).wait_recv()
        grad = grad + dot_nt(goth[g], w_far[g])
        gradt = gradt + dot_nt(w_far[g], goth[g])
    for g in range(pairs):
        da[g] = grad[:, cols(g)].astype(BF16)
    products = gradt.astype(BF16).astype(F32) * atr[...]
    for h in range(heads):
        stats[heads + h:heads + h + 1, :] = jnp.sum(products[head_rows(h)], axis=0, keepdims=True)
    s_down.send(0)
    for g in range(pairs):
        a_down[g].send(0)
    for h in range(heads):
        am[h] = only(da[h // 2], h)

    def query_pair(slot, g, kblk, vblk, masked_a, tops, dots, grad_q, first, own=False):
        ktr = kblk.astype(F32).T.astype(BF16)
        sums = []
        for h in (2 * g, 2 * g + 1):
            weights = jnp.exp2(kept[slot, h] - tops(h))
            pushes = dot_nt(vblk, masked_a[h])
            slopes = (weights * (pushes - dots(h))).astype(BF16)
            part = dot_nn(ktr[head_rows(h - 2 * g)], slopes)
            grad_q[head_rows(h), :] = part if first else grad_q[head_rows(h), :] + part
            if own:
                sums.append((dot_nn(slopes, q_ref[:, cols(g)]),
                             dot_nn(weights.astype(BF16), da[g])))
        if own:
            dkacc[:, cols(g)] = jnp.where(low, sums[0][0], sums[1][0])
            dvacc[:, cols(g)] = jnp.where(low, sums[0][1], sums[1][1])

    own_rows = (lambda h: stats[h:h + 1, :], lambda h: stats[heads + h:heads + h + 1, :])
    far_rows = (lambda h: sbuf[1, h:h + 1, :], lambda h: sbuf[1, heads + h:heads + h + 1, :])

    for g in range(pairs):
        query_pair(0, g, kv_ref[g, 0], kv_ref[g, 1], am, *own_rows, dqt, True, True)

    def own_queries(i):
        @pl.when(s - i >= 0)
        def _():
            for g in range(pairs):
                query_pair(i, g, kvbuf[g, i - 1, 0], kvbuf[g, i - 1, 1], am, *own_rows, dqt, False)

    def key_pair(j, g):
        qblk, ablk, far = qbuf[j - 1, :, cols(g)], abuf[g, j - 1], sbuf[j - 1]
        sums = []
        for h in (2 * g, 2 * g + 1):
            scores = dot_nt(km[h], qblk) * to_log2 + bias[reach + j]
            weights = jnp.exp2(scores - far[h:h + 1, :])
            pushes = dot_nt(vm[h], ablk)
            slopes = (weights * (pushes - far[heads + h:heads + h + 1, :])).astype(BF16)
            sums.append((dot_nn(slopes, qblk), dot_nn(weights.astype(BF16), ablk)))
        dkacc[:, cols(g)] = dkacc[:, cols(g)] + jnp.where(low, sums[0][0], sums[1][0])
        dvacc[:, cols(g)] = dvacc[:, cols(g)] + jnp.where(low, sums[0][1], sums[1][1])

    def forward_grad(j):
        s_down.forward(j)
        for g in range(pairs):
            a_down[g].forward(j)

    def keys_even(j):
        @pl.when(s + j < shards)
        def _():
            for g in range(pairs):
                key_pair(j, g)

    def keys_odd(j):
        @pl.when(s + j < shards)
        def _():
            s_down.wait(j)
            q_down.wait(j)
            for g in range(pairs):
                a_down[g].wait(j)
                key_pair(j, g)

    def far_grads(both):
        for g in range(pairs):
            for h in (2 * g, 2 * g + 1):
                afar[h] = only(abuf[g, 1], h)
            for d in (near - 1, near)[:2 if both else 1]:
                query_pair(d + 2, g, kvbuf[g, d - 1, 0], kvbuf[g, d - 1, 1], afar, *far_rows, dfar, d < near)
            part_dq[g] = dfar[cols(g), :].astype(BF16)
            far_grad_copy(g).start()

    if near == 2:
        own_queries(1)
        own_queries(2)
    else:
        pl.loop(1, near + 1)(own_queries)

    forward_grad(2)

    @pl.when(helps & (s == near - 1))
    def _():
        far_grads(False)

    keys_even(2)
    keys_odd(1)
    forward_grad(4)

    @pl.when(helps & (s >= near))
    def _():
        far_grads(True)

    keys_even(4)
    keys_odd(3)

    if reach > 4:
        @pl.loop(3, reach // 2 + 1)
        def _(i):
            forward_grad(2 * i)
            keys_even(2 * i)
            keys_odd(2 * i - 1)

    @pl.when(helped)
    def _():
        for g in range(pairs):
            far_grad_copy(g).wait_recv()
            dqt[cols(g), :] = dqt[cols(g), :] + far_dq[g].astype(F32)

    gq_ref[...] = (dqt[...] * scale).T.astype(BF16)
    gk_ref[...] = (dkacc[...] * scale).astype(BF16)
    gv_ref[...] = dvacc[...].astype(BF16)

    flat = (*kv_up, q_down, *a_down, s_down)
    for relay in flat:
        relay.finish(0)

    @pl.loop(1, reach // 2 + 1)
    def _(i):
        for relay in flat:
            relay.finish(2 * i)

    @pl.when(helps)
    def _():
        for g in range(pairs):
            for copy in (*far_copies(g), far_grad_copy(g)):
                copy.wait_send()

    w_copy.wait_send()
    for g in range(pairs):
        pair_copy(1 + g, aown.at[g], aoth.at[g]).wait_send()
        pair_copy(1 + pairs + g, gown.at[g], goth.at[g]).wait_send()

    @pl.when(has_prev)
    def _():
        cot_copy.wait_send()
        first_copy.wait_send()

    @pl.when(has_next)
    def _():
        last_copy.wait_send()


def store_kernel(*refs):
    count = len(refs) // 2
    stores = [pltpu.make_async_copy(refs[index], refs[count + index], refs[-1].at[index])
              for index in range(count)]
    for store in stores:
        store.start()
    for store in stores:
        store.wait()


def local(queries, keys, values, residual_in, out_proj, conv_kernel, valid_counts, segment_ids,
          cotangent):
    rows, width = queries.shape
    heads = width // HEAD_DIM
    pairs = width // PAIR
    shards = valid_counts.shape[0]
    window = segment_ids.shape[0]
    reach = -(-(window // 2) // rows)
    block = (rows, width)
    sems = pltpu.SemaphoreType.DMA
    near = reach - 2
    part_rows = (pairs, PAIR, rows)

    def relay_sems(span, parts=()):
        return [sems(parts + (span,)), sems(parts + (span // 2 + 1,)), sems(parts + (span // 2 + 1,))]

    scratch = [pltpu.VMEM(block, BF16), pltpu.VMEM((pairs, 2, rows, PAIR), BF16),
               pltpu.VMEM(block, BF16)] + [
        pltpu.VMEM(out_proj.shape, BF16), pltpu.VMEM(conv_kernel.shape, BF16),
        pltpu.VMEM(block, BF16), pltpu.VMEM((shards, rows), jnp.int32),
        pltpu.SemaphoreType.DMA((5,)), pltpu.SemaphoreType.DMA((pairs, 2)),
        pltpu.SemaphoreType.DMA((shards,)),
        pltpu.VMEM((pairs, near, 2, rows, PAIR), BF16),
        pltpu.VMEM((reach,) + block, BF16), pltpu.VMEM((pairs, reach, rows, PAIR), BF16),
        pltpu.VMEM((reach, 2 * heads, rows), F32),
        pltpu.VMEM(block, BF16),
        pltpu.VMEM((pairs, rows, PAIR), BF16), pltpu.VMEM((pairs, rows, PAIR), BF16),
        pltpu.VMEM((pairs, rows, PAIR), BF16),
        pltpu.VMEM(block, BF16), pltpu.VMEM((HALO, width), BF16), pltpu.VMEM((HALO, width), BF16),
        pltpu.VMEM((HALO, width), BF16),
        pltpu.VMEM((2 * reach + 1, rows, rows), F32), pltpu.VMEM((reach + 1, heads, rows, rows), F32), pltpu.VMEM((rows, 128), F32),
        pltpu.VMEM((heads, rows, PAIR), BF16), pltpu.VMEM((heads, rows, PAIR), BF16),
        pltpu.VMEM((heads, rows, PAIR), BF16), pltpu.VMEM((heads, rows, PAIR), BF16),
        pltpu.VMEM((width, rows), F32), pltpu.VMEM((2 * heads, rows), F32),
        pltpu.VMEM((width, rows), F32), pltpu.VMEM((width, rows), F32),
        pltpu.VMEM(block, F32), pltpu.VMEM(block, F32),
        pltpu.VMEM((pairs, rows, PAIR), BF16), pltpu.VMEM((rows + 2 * HALO, width), F32),
        pltpu.VMEM((8, rows + 2 * HALO, width), F32), pltpu.VMEM((8, rows + HALO, width), F32),
        pltpu.VMEM((rows + HALO + 8, width), F32),
        pltpu.VMEM((pairs, rows, PAIR), BF16),
        pltpu.VMEM((heads, rows, PAIR), BF16), pltpu.VMEM((heads, rows, PAIR), BF16),
        pltpu.VMEM((width, rows), F32), pltpu.VMEM((width, rows), F32),
        pltpu.VMEM(part_rows, BF16), pltpu.VMEM((pairs, 8, rows), F32),
        pltpu.VMEM(part_rows, BF16), pltpu.VMEM((pairs, 8, rows), F32),
        pltpu.VMEM(part_rows, BF16), pltpu.VMEM(part_rows, BF16),
    ] + relay_sems(near, (pairs,)) + relay_sems(reach) + relay_sems(reach, (pairs,)) + relay_sems(reach) + [
        pltpu.SemaphoreType.DMA((1 + 2 * pairs,)), pltpu.SemaphoreType.DMA((1 + 2 * pairs,)),
        pltpu.SemaphoreType.DMA((3,)), pltpu.SemaphoreType.DMA((3,)),
        pltpu.SemaphoreType.DMA((3 * pairs,)), pltpu.SemaphoreType.DMA((3 * pairs,)),
    ]
    vmem = pl.BlockSpec(memory_space=pltpu.VMEM)
    hbm = pl.BlockSpec(memory_space=pltpu.MemorySpace.HBM)
    results = pl.pallas_call(
        functools.partial(kernel, shards, reach, heads),
        out_shape=(pltpu.VMEM(block, BF16),) * 5,
        in_specs=[pl.BlockSpec(memory_space=pltpu.SMEM)] + [hbm] * 8,
        out_specs=(vmem,) * 5,
        scratch_shapes=scratch,
        compiler_params=pltpu.CompilerParams(
            collective_id=0, has_side_effects=True, vmem_limit_bytes=VMEM_BYTES),
    )(valid_counts, segment_ids, queries, keys, values, residual_in, out_proj,
      conv_kernel, cotangent)
    return pl.pallas_call(
        store_kernel,
        out_shape=(jax.ShapeDtypeStruct(block, BF16),) * 5,
        in_specs=[pl.BlockSpec(memory_space=pl.ANY)] * 5,
        out_specs=(hbm,) * 5,
        scratch_shapes=[pltpu.SemaphoreType.DMA((5,))],
    )(*[pltpu.with_memory_space_constraint(r, pltpu.VMEM) for r in results])


def solution(mesh):
    tokens = P(("groups", "tm"), "mp")
    in_specs = (tokens, tokens, tokens, tokens, P("mp", None), P(None, "mp"), P("groups"),
                P("groups"), tokens)
    return jax.shard_map(local, mesh=mesh, in_specs=in_specs, out_specs=(tokens,) * 5,
                         check_vma=False)
```

```python
import functools
import math

import jax
import jax.numpy as jnp
from jax import lax
from jax.experimental import pallas as pl
from jax.experimental.pallas import tpu as pltpu
from jax.sharding import PartitionSpec as P

HEAD_DIM = 64
PAIR = 2 * HEAD_DIM
HALO = 32
VMEM_BYTES = 63 * 1024 * 1024
LOG2E = math.log2(math.e)
MASKED = -1e30
MESH = pl.DeviceIdType.MESH
F32, BF16 = jnp.float32, jnp.bfloat16


def dot_nt(a, b):
    return lax.dot_general(a, b, (((1,), (1,)), ((), ())), preferred_element_type=F32)


def dot_nn(a, b):
    return jnp.dot(a, b, preferred_element_type=F32)


class Relay:
    def __init__(self, own, slot, recv, send_z, send_y, s, shards, reach, direction):
        self.own, self.slot, self.recv = own, slot, recv
        self.send_z, self.send_y = send_z, send_y
        self.s, self.shards, self.reach, self.direction = s, shards, reach, direction
        odd = lax.rem(s, 2)
        self.lead = odd == (0 if direction > 0 else 1)
        self.partner = s + 1 - 2 * odd
        self.target = s + 2 * direction
        self.has_target = (s + 2 < shards) if direction > 0 else (s >= 2)

    def exists(self, j):
        return (self.s - j >= 0) if self.direction > 0 else (self.s + j < self.shards)

    def source(self, j):
        return self.own if isinstance(j, int) and j == 0 else self.slot(j)

    def z_copy(self, j):
        return pltpu.make_async_remote_copy(
            src_ref=self.source(j), dst_ref=self.slot(j + 2),
            send_sem=self.send_z.at[j // 2], recv_sem=self.recv.at[j + 1],
            device_id={"tm": self.target}, device_id_type=MESH)

    def y_copy(self, j, landing):
        return pltpu.make_async_remote_copy(
            src_ref=self.source(j), dst_ref=self.slot(landing),
            send_sem=self.send_y.at[j // 2], recv_sem=self.recv.at[landing - 1],
            device_id={"tm": self.partner}, device_id_type=MESH)

    def each(self, j, act, along="zy"):
        at_start = isinstance(j, int) and j == 0
        here = self.exists(j)

        if "z" in along:
            @pl.when(here & self.has_target & (j <= self.reach - 2))
            def _():
                act(self.z_copy(j))

        if "y" not in along:
            return

        @pl.when(here & self.lead & (j <= self.reach - 2))
        def _():
            act(self.y_copy(j, j + 1))

        if not at_start:
            @pl.when(here & jnp.logical_not(self.lead))
            def _():
                act(self.y_copy(j, j - 1))

    def send(self, j, along="zy"):
        self.each(j, lambda copy: copy.start(), along)

    def forward(self, j, along="zy"):
        @pl.when(self.exists(j))
        def _():
            self.wait(j)
            self.send(j, along)

    def finish(self, j):
        @pl.when(j <= self.reach)
        def _():
            self.each(j, lambda copy: copy.wait_send())

    def wait(self, j):
        pltpu.make_async_remote_copy(
            src_ref=self.slot(j), dst_ref=self.slot(j),
            send_sem=self.send_z.at[0], recv_sem=self.recv.at[j - 1],
            device_id={"tm": self.partner}, device_id_type=MESH).wait_recv()


def kernel(shards, reach, heads,
           counts_in, seg_in, q_in, k_in, v_in, res_in, w_in, taps_in, cot_in,
           out_ref, gin_ref, gq_ref, gk_ref, gv_ref,
           q_ref, kv_ref, res_ref, w_ref, taps_ref, cot_ref, counts_ref, seg_ref, load_sem, kv_sem, seg_sem,
           kvbuf, qbuf, abuf, sbuf, woth, aown, aoth, goth,
           hid, prev, nxt, cnext,
           bias, kept, colown, qm, km, vm, am, otr, stats, atr, dqt, dkacc, dvacc,
           da, ext, shifted, spread, gconv, gown,
           qfar, afar, ofar, dfar, part_out, part_stats, far_out, far_stats, part_dq, far_dq,
           kvrecv, kvz, kvy, qrecv, qz, qy, arecv, az, ay, srecv, sz, sy,
           pair_send, pair_recv, halo_send, halo_recv, far_send, far_recv):
    rows, width = q_ref.shape
    pairs = width // PAIR
    kv_loads = [pltpu.make_async_copy(src.at[:, g * PAIR:(g + 1) * PAIR], kv_ref.at[g, index],
                                      kv_sem.at[g, index])
                for g in range(pairs) for index, src in enumerate((k_in, v_in))]
    loads = [pltpu.make_async_copy(src, dst, load_sem.at[index])
             for index, (src, dst) in enumerate((
                 (q_in, q_ref), (res_in, res_ref), (w_in, w_ref),
                 (taps_in, taps_ref), (cot_in, cot_ref), (counts_in, counts_ref)))]
    seg_loads = [pltpu.make_async_copy(seg_in.at[pl.ds(shard * rows, rows)], seg_ref.at[shard],
                                       seg_sem) for shard in range(shards)]
    for load in kv_loads + loads + seg_loads:
        load.start()
    s = lax.axis_index("tm")
    mp = lax.axis_index("mp")
    other = 1 - mp
    odd = lax.rem(s, 2)
    scale = HEAD_DIM ** -0.5
    to_log2 = scale * LOG2E

    barrier = pltpu.get_barrier_semaphore()
    for shift in (-2, -1, 1, 2):
        @pl.when((s + shift >= 0) & (s + shift < shards))
        def _():
            pl.semaphore_signal(barrier, inc=1, device_id={"tm": s + shift}, device_id_type=MESH)
    pl.semaphore_signal(barrier, inc=1, device_id={"mp": other}, device_id_type=MESH)
    peers = jnp.minimum(s, 2) + jnp.minimum(shards - 1 - s, 2) + 1
    pl.semaphore_wait(barrier, peers)

    near = reach - 2

    def part_relays(own, buf, sems, span, direction):
        return [Relay(own.at[g], lambda j, g=g: buf.at[g, j - 1], *(sem.at[g] for sem in sems),
                      s, shards, span, direction) for g in range(pairs)]

    kv_up = part_relays(kv_ref, kvbuf, (kvrecv, kvz, kvy), near, 1)
    q_down = Relay(q_in, lambda j: qbuf.at[j - 1], qrecv, qz, qy, s, shards, reach, -1)
    a_down = part_relays(da, abuf, (arecv, az, ay), reach, -1)
    s_down = Relay(stats, lambda j: sbuf.at[j - 1], srecv, sz, sy, s, shards, reach, -1)

    for load in kv_loads:
        load.wait()
    for g in range(pairs):
        kv_up[g].send(0)
        if g == 0:
            q_down.send(0, "z")

    helps = (s + 2 < shards) & (s >= reach - 3)
    helped = s >= reach - 1

    def far_copy(index, src, dst):
        return pltpu.make_async_remote_copy(
            src_ref=src, dst_ref=dst, send_sem=far_send.at[index], recv_sem=far_recv.at[index],
            device_id={"tm": s + 2}, device_id_type=MESH)

    def far_copies(g):
        return (far_copy(3 * g, part_out.at[g], far_out.at[g]),
                far_copy(3 * g + 1, part_stats.at[g], far_stats.at[g]))

    def far_grad_copy(g):
        return far_copy(3 * g + 2, part_dq.at[g], far_dq.at[g])

    def pair_copy(index, src, dst):
        return pltpu.make_async_remote_copy(
            src_ref=src, dst_ref=dst, send_sem=pair_send.at[index], recv_sem=pair_recv.at[index],
            device_id={"mp": other}, device_id_type=MESH)

    own_cols = pl.ds(pl.multiple_of(mp * width, width), width)
    other_cols = pl.ds(pl.multiple_of(other * width, width), width)
    w_copy = pair_copy(0, w_in.at[:, other_cols], woth)
    w_copy.start()

    def halo_copy(index, src, dst, shift):
        return pltpu.make_async_remote_copy(
            src_ref=src, dst_ref=dst, send_sem=halo_send.at[index], recv_sem=halo_recv.at[index],
            device_id={"tm": s + shift}, device_id_type=MESH)

    has_prev, has_next = s > 0, s < shards - 1
    cot_copy = halo_copy(0, cot_in.at[pl.ds(0, HALO)], cnext, -1)
    last_copy = halo_copy(1, hid.at[pl.ds(rows - HALO, HALO)], prev, 1)
    first_copy = halo_copy(2, hid.at[pl.ds(0, HALO)], nxt, -1)

    @pl.when(has_prev)
    def _():
        cot_copy.start()

    @pl.when(jnp.logical_not(has_prev))
    def _():
        prev[...] = jnp.zeros_like(prev)

    @pl.when(jnp.logical_not(has_next))
    def _():
        nxt[...] = jnp.zeros_like(nxt)
        cnext[...] = jnp.zeros_like(cnext)

    for load in loads:
        load.wait()
    pltpu.make_async_copy(seg_ref, seg_ref, seg_sem).wait()

    lane = lax.broadcasted_iota(jnp.int32, (rows, PAIR), 1)
    low = lane < HEAD_DIM

    def only(block, h):
        keep = low if h % 2 == 0 else jnp.logical_not(low)
        return jnp.where(keep, block.astype(F32), 0.0).astype(BF16)

    def cols(g):
        return slice(g * PAIR, (g + 1) * PAIR)

    def head_rows(h):
        return slice(h * HEAD_DIM, (h + 1) * HEAD_DIM)

    for h in range(heads):
        qm[h] = only(q_ref[:, cols(h // 2)], h)
        km[h] = only(kv_ref[h // 2, 0], h)
        vm[h] = only(kv_ref[h // 2, 1], h)

    def seg_row(shard):
        return seg_ref[pl.ds(shard, 1), :]

    def label_col(shard):
        position = lax.broadcasted_iota(jnp.int32, (1, rows), 1)
        label = jnp.where(position < counts_ref[shard], seg_row(shard), -1).astype(F32)
        return jnp.broadcast_to(label, (128, rows)).T

    own_seg = seg_row(s).astype(F32)

    def fill_bias(slot, col, segs, diagonal):
        for part in range(rows // 128):
            at = slice(part * 128, (part + 1) * 128)
            seen = col == segs[:, at]
            if diagonal:
                key_at = lax.broadcasted_iota(jnp.int32, (rows, 128), 0)
                query_at = lax.broadcasted_iota(jnp.int32, (rows, 128), 1) + part * 128
                seen = (seen & (key_at < query_at)) | (key_at == query_at)
            bias[slot, :, at] = jnp.where(seen, 0.0, MASKED)

    colown[...] = label_col(s)
    fill_bias(0, colown[...], own_seg, True)

    def forward_pair(g, kblk, vblk, targets):
        vtr = vblk.astype(F32).T.astype(BF16)
        for slot, masked_q, totals, out, first in targets:
            for h in (2 * g, 2 * g + 1):
                at_top, at_mass = totals(h)
                scores = dot_nt(kblk, masked_q[h]) * to_log2 + bias[slot]
                kept[slot, h] = scores
                top = jnp.max(scores, axis=0, keepdims=True)
                if not first:
                    top = jnp.maximum(at_top[...], top)
                weights = jnp.exp2(scores - top)
                mass = jnp.sum(weights, axis=0, keepdims=True)
                part = dot_nn(vtr[head_rows(h - 2 * g)], weights.astype(BF16))
                if not first:
                    fade = jnp.exp2(at_top[...] - top)
                    mass = mass + at_mass[...] * fade
                    part = part + out[head_rows(h), :] * fade
                at_top[...] = top
                at_mass[...] = mass
                out[head_rows(h), :] = part

    def own_totals(h):
        return stats.at[h:h + 1, :], stats.at[heads + h:heads + h + 1, :]

    def far_totals(h):
        g, at = h // 2, h % 2
        return part_stats.at[g, at:at + 1, :], part_stats.at[g, 2 + at:3 + at, :]

    def own_target(slot, first=False):
        return slot, qm, own_totals, otr, first

    def far_target(slot):
        return slot, qfar, far_totals, ofar, False

    for g in range(pairs):
        forward_pair(g, kv_ref[g, 0], kv_ref[g, 1], [own_target(0, True)])
        part_stats[g, 0:2, :] = jnp.full((2, rows), 2 * MASKED, F32)
        part_stats[g, 2:, :] = jnp.zeros((6, rows), F32)
    ofar[...] = jnp.zeros_like(ofar)

    def own_step(i):
        return jnp.where(odd == 1, i, jnp.where(lax.rem(i, 2) == 1, i + 1, i - 1))

    if near > 2:
        @pl.loop(1, near - 1)
        def _(i):
            j = own_step(i)

            @pl.when(s - j >= 0)
            def _():
                fill_bias(j, label_col(s - j), own_seg, False)

            for g in range(pairs):
                @pl.when(lax.rem(i, 2) == 1)
                def _():
                    kv_up[g].forward(i + 1)

                @pl.when(s - j >= 0)
                def _():
                    @pl.when(lax.rem(j, 2) == 1)
                    def _():
                        kv_up[g].wait(j)

                    forward_pair(g, kvbuf[g, j - 1, 0], kvbuf[g, j - 1, 1], [own_target(j)])

    for d in (near - 1, near):
        @pl.when(s - d >= 0)
        def _():
            col = label_col(s - d)
            fill_bias(d, col, own_seg, False)
            fill_bias(d + 2, col, seg_row(jnp.minimum(s + 2, shards - 1)).astype(F32), False)

    q_down.forward(2, "z")
    for j in range(1, reach + 1):
        @pl.when(s + j < shards)
        def _():
            fill_bias(reach + j, colown[...], seg_row(s + j).astype(F32), False)

    for g in range(pairs):
        @pl.when(helps)
        def _():
            for h in (2 * g, 2 * g + 1):
                qfar[h] = only(qbuf[1, :, cols(g)], h)

        kv_up[g].forward(near)
        for step in (near - 1, near):
            j = own_step(step)

            @pl.when(s - j >= 0)
            def _():
                @pl.when(lax.rem(j, 2) == 1)
                def _():
                    kv_up[g].wait(j)

                forward_pair(g, kvbuf[g, j - 1, 0], kvbuf[g, j - 1, 1], [far_target(j + 2), own_target(j)])

        @pl.when(helps)
        def _():
            part_out[g] = ofar[cols(g), :].astype(BF16)
            for copy in far_copies(g):
                copy.start()

    for g in range(pairs):
        @pl.when(helped)
        def _():
            for copy in far_copies(g):
                copy.wait_recv()
            for at in (0, 1):
                h = 2 * g + at
                at_top, at_mass = own_totals(h)
                far_top = far_stats[g, at:at + 1, :]
                top = jnp.maximum(at_top[...], far_top)
                fade, far_fade = jnp.exp2(at_top[...] - top), jnp.exp2(far_top - top)
                at_top[...] = top
                at_mass[...] = at_mass[...] * fade + far_stats[g, 2 + at:3 + at, :] * far_fade
                far_part = far_out[g, head_rows(at), :].astype(F32)
                otr[head_rows(h), :] = otr[head_rows(h), :] * fade + far_part * far_fade

        for h in (2 * g, 2 * g + 1):
            atr[head_rows(h), :] = otr[head_rows(h), :] / stats[heads + h:heads + h + 1, :]
        block = atr[cols(g), :]
        aown[g] = block.T.astype(BF16)
        atr[cols(g), :] = block.astype(BF16).astype(F32)
        pair_copy(1 + g, aown.at[g], aoth.at[g]).start()
    for h in range(heads):
        stats[h:h + 1, :] = stats[h:h + 1, :] + jnp.log(stats[heads + h:heads + h + 1, :]) * LOG2E

    mixed = res_ref[...].astype(F32)
    w_own = w_ref[:, own_cols]
    for g in range(pairs):
        mixed = mixed + dot_nn(aown[g], w_own[cols(g), :])
    w_copy.wait_recv()
    for g in range(pairs):
        pair_copy(1 + g, aown.at[g], aoth.at[g]).wait_recv()
        mixed = mixed + dot_nn(aoth[g], woth[cols(g), :])
    hid[...] = mixed.astype(BF16)

    @pl.when(has_next)
    def _():
        last_copy.start()

    @pl.when(has_prev)
    def _():
        first_copy.start()

    q_down.send(0, "y")
    q_down.send(2, "y")

    @pl.loop(2, reach // 2 + 1)
    def _(i):
        q_down.forward(2 * i)

    long = rows + HALO
    tap_count = taps_ref.shape[0]
    taps = taps_ref[...].astype(F32)

    def shift_hidden(start, stop):
        for r in range(8):
            shifted[r, start:stop, :] = ext[start - r:stop - r, :]

    def shift_grad(start, stop):
        for r in range(8):
            spread[r, start:stop, :] = gconv[start + r:stop + r, :]

    def convolve(g, start, stop):
        size = stop - start
        mix = jnp.zeros((size, PAIR), F32)
        for tap in range(tap_count):
            at = HALO + start - 8 * (tap // 8)
            mix = mix + taps[tap:tap + 1, cols(g)] * shifted[tap % 8, at:at + size, cols(g)]
        gate = jax.nn.sigmoid(mix)
        if start < rows:
            up = cot_ref[start:stop, cols(g)].astype(F32)
            hidden = ext[HALO + start:HALO + stop, cols(g)]
            out_ref[start:stop, cols(g)] = (hidden + mix * gate).astype(BF16)
        else:
            up = cnext[:, cols(g)].astype(F32)
        gconv[start:stop, cols(g)] = up * gate * (1.0 + mix * (1.0 - gate))

    def convolve_back(g, start, stop):
        grad = cot_ref[start:stop, cols(g)].astype(F32)
        for tap in range(tap_count):
            at = start + 8 * (tap // 8)
            grad = grad + taps[tap:tap + 1, cols(g)] * spread[tap % 8, at:at + stop - start, cols(g)]
        gown[g, start:stop, :] = grad.astype(BF16)

    ext[HALO:HALO + rows, :] = hid[...].astype(F32)
    gconv[long:, :] = jnp.zeros((8, width), F32)
    shift_hidden(HALO + 8, HALO + rows)
    step, back_step = (rows - HALO) // 2, (rows - 2 * HALO) // 2
    for g in range(pairs):
        for start in range(HALO, rows, step):
            convolve(g, start, start + step)
    shift_grad(HALO, rows - 8)
    for g in range(pairs):
        for start in range(HALO, rows - HALO, back_step):
            convolve_back(g, start, start + back_step)

    @pl.when(has_next)
    def _():
        first_copy.wait_recv()
        cot_copy.wait_recv()

    @pl.when(has_prev)
    def _():
        last_copy.wait_recv()

    ext[0:HALO, :] = prev[...].astype(F32)
    ext[HALO + rows:, :] = nxt[...].astype(F32)
    shift_hidden(8, HALO + 8)
    shift_hidden(HALO + rows, long + HALO)
    for g in range(pairs):
        convolve(g, 0, HALO)
        convolve(g, rows, long)
    shift_grad(0, HALO)
    shift_grad(rows - 8, long)
    for g in range(pairs):
        convolve_back(g, 0, HALO)
        convolve_back(g, rows - HALO, rows)
        gin_ref[:, cols(g)] = gown[g]
        pair_copy(1 + pairs + g, gown.at[g], goth.at[g]).start()

    w_mine = [w_ref[:, pl.ds(pl.multiple_of(mp * width + g * PAIR, PAIR), PAIR)] for g in range(pairs)]
    w_far = [w_ref[:, pl.ds(pl.multiple_of(other * width + g * PAIR, PAIR), PAIR)] for g in range(pairs)]
    grad = dot_nt(gown[0], w_mine[0])
    gradt = dot_nt(w_mine[0], gown[0])
    for g in range(1, pairs):
        grad = grad + dot_nt(gown[g], w_mine[g])
        gradt = gradt + dot_nt(w_mine[g], gown[g])
    for g in range(pairs):
        pair_copy(1 + pairs + g, gown.at[g], goth.at[g]).wait_recv()
        grad = grad + dot_nt(goth[g], w_far[g])
        gradt = gradt + dot_nt(w_far[g], goth[g])
    for g in range(pairs):
        da[g] = grad[:, cols(g)].astype(BF16)
    products = gradt.astype(BF16).astype(F32) * atr[...]
    for h in range(heads):
        stats[heads + h:heads + h + 1, :] = jnp.sum(products[head_rows(h)], axis=0, keepdims=True)
    s_down.send(0)
    for g in range(pairs):
        a_down[g].send(0)
    for h in range(heads):
        am[h] = only(da[h // 2], h)

    def query_pair(slot, g, kblk, vblk, masked_a, tops, dots, grad_q, first, own=False):
        ktr = kblk.astype(F32).T.astype(BF16)
        sums = []
        for h in (2 * g, 2 * g + 1):
            weights = jnp.exp2(kept[slot, h] - tops(h))
            pushes = dot_nt(vblk, masked_a[h])
            slopes = (weights * (pushes - dots(h))).astype(BF16)
            part = dot_nn(ktr[head_rows(h - 2 * g)], slopes)
            grad_q[head_rows(h), :] = part if first else grad_q[head_rows(h), :] + part
            if own:
                sums.append((dot_nn(slopes, q_ref[:, cols(g)]),
                             dot_nn(weights.astype(BF16), da[g])))
        if own:
            dkacc[:, cols(g)] = jnp.where(low, sums[0][0], sums[1][0])
            dvacc[:, cols(g)] = jnp.where(low, sums[0][1], sums[1][1])

    own_rows = (lambda h: stats[h:h + 1, :], lambda h: stats[heads + h:heads + h + 1, :])
    far_rows = (lambda h: sbuf[1, h:h + 1, :], lambda h: sbuf[1, heads + h:heads + h + 1, :])

    for g in range(pairs):
        query_pair(0, g, kv_ref[g, 0], kv_ref[g, 1], am, *own_rows, dqt, True, True)

    def own_queries(i):
        @pl.when(s - i >= 0)
        def _():
            for g in range(pairs):
                query_pair(i, g, kvbuf[g, i - 1, 0], kvbuf[g, i - 1, 1], am, *own_rows, dqt, False)

    def key_pair(j, g):
        qblk, ablk, far = qbuf[j - 1, :, cols(g)], abuf[g, j - 1], sbuf[j - 1]
        sums = []
        for h in (2 * g, 2 * g + 1):
            scores = dot_nt(km[h], qblk) * to_log2 + bias[reach + j]
            weights = jnp.exp2(scores - far[h:h + 1, :])
            pushes = dot_nt(vm[h], ablk)
            slopes = (weights * (pushes - far[heads + h:heads + h + 1, :])).astype(BF16)
            sums.append((dot_nn(slopes, qblk), dot_nn(weights.astype(BF16), ablk)))
        dkacc[:, cols(g)] = dkacc[:, cols(g)] + jnp.where(low, sums[0][0], sums[1][0])
        dvacc[:, cols(g)] = dvacc[:, cols(g)] + jnp.where(low, sums[0][1], sums[1][1])

    def forward_grad(j):
        s_down.forward(j)
        for g in range(pairs):
            a_down[g].forward(j)

    def keys_even(j):
        @pl.when(s + j < shards)
        def _():
            for g in range(pairs):
                key_pair(j, g)

    def keys_odd(j):
        @pl.when(s + j < shards)
        def _():
            s_down.wait(j)
            q_down.wait(j)
            for g in range(pairs):
                a_down[g].wait(j)
                key_pair(j, g)

    def far_grads(both):
        for g in range(pairs):
            for h in (2 * g, 2 * g + 1):
                afar[h] = only(abuf[g, 1], h)
            for d in (near - 1, near)[:2 if both else 1]:
                query_pair(d + 2, g, kvbuf[g, d - 1, 0], kvbuf[g, d - 1, 1], afar, *far_rows, dfar, d < near)
            part_dq[g] = dfar[cols(g), :].astype(BF16)
            far_grad_copy(g).start()

    if near == 2:
        own_queries(1)
        own_queries(2)
    else:
        pl.loop(1, near + 1)(own_queries)

    def far_step(parity):
        @pl.when(helps & (odd == parity) & (s >= near))
        def _():
            far_grads(True)

        if (near - 1) % 2 == parity:
            @pl.when(helps & (s == near - 1))
            def _():
                far_grads(False)

    forward_grad(2)
    far_step(1)
    keys_even(2)
    keys_odd(1)
    forward_grad(4)
    far_step(0)
    keys_even(4)
    keys_odd(3)

    if reach > 4:
        @pl.loop(3, reach // 2 + 1)
        def _(i):
            forward_grad(2 * i)
            keys_even(2 * i)
            keys_odd(2 * i - 1)

    @pl.when(helped)
    def _():
        for g in range(pairs):
            far_grad_copy(g).wait_recv()
            dqt[cols(g), :] = dqt[cols(g), :] + far_dq[g].astype(F32)

    gq_ref[...] = (dqt[...] * scale).T.astype(BF16)
    gk_ref[...] = (dkacc[...] * scale).astype(BF16)
    gv_ref[...] = dvacc[...].astype(BF16)

    flat = (*kv_up, q_down, *a_down, s_down)
    for relay in flat:
        relay.finish(0)

    @pl.loop(1, reach // 2 + 1)
    def _(i):
        for relay in flat:
            relay.finish(2 * i)

    @pl.when(helps)
    def _():
        for g in range(pairs):
            for copy in (*far_copies(g), far_grad_copy(g)):
                copy.wait_send()

    w_copy.wait_send()
    for g in range(pairs):
        pair_copy(1 + g, aown.at[g], aoth.at[g]).wait_send()
        pair_copy(1 + pairs + g, gown.at[g], goth.at[g]).wait_send()

    @pl.when(has_prev)
    def _():
        cot_copy.wait_send()
        first_copy.wait_send()

    @pl.when(has_next)
    def _():
        last_copy.wait_send()


def store_kernel(*refs):
    count = len(refs) // 2
    stores = [pltpu.make_async_copy(refs[index], refs[count + index], refs[-1].at[index])
              for index in range(count)]
    for store in stores:
        store.start()
    for store in stores:
        store.wait()


def local(queries, keys, values, residual_in, out_proj, conv_kernel, valid_counts, segment_ids,
          cotangent):
    rows, width = queries.shape
    heads = width // HEAD_DIM
    pairs = width // PAIR
    shards = valid_counts.shape[0]
    window = segment_ids.shape[0]
    reach = -(-(window // 2) // rows)
    block = (rows, width)
    sems = pltpu.SemaphoreType.DMA
    near = reach - 2
    part_rows = (pairs, PAIR, rows)

    def relay_sems(span, parts=()):
        return [sems(parts + (span,)), sems(parts + (span // 2 + 1,)), sems(parts + (span // 2 + 1,))]

    scratch = [pltpu.VMEM(block, BF16), pltpu.VMEM((pairs, 2, rows, PAIR), BF16),
               pltpu.VMEM(block, BF16)] + [
        pltpu.VMEM(out_proj.shape, BF16), pltpu.VMEM(conv_kernel.shape, BF16),
        pltpu.VMEM(block, BF16), pltpu.SMEM(valid_counts.shape, jnp.int32),
        pltpu.VMEM((shards, rows), jnp.int32),
        pltpu.SemaphoreType.DMA((6,)), pltpu.SemaphoreType.DMA((pairs, 2)), pltpu.SemaphoreType.DMA,
        pltpu.VMEM((pairs, near, 2, rows, PAIR), BF16),
        pltpu.VMEM((reach,) + block, BF16), pltpu.VMEM((pairs, reach, rows, PAIR), BF16),
        pltpu.VMEM((reach, 2 * heads, rows), F32),
        pltpu.VMEM(block, BF16),
        pltpu.VMEM((pairs, rows, PAIR), BF16), pltpu.VMEM((pairs, rows, PAIR), BF16),
        pltpu.VMEM((pairs, rows, PAIR), BF16),
        pltpu.VMEM(block, BF16), pltpu.VMEM((HALO, width), BF16), pltpu.VMEM((HALO, width), BF16),
        pltpu.VMEM((HALO, width), BF16),
        pltpu.VMEM((2 * reach + 1, rows, rows), F32), pltpu.VMEM((reach + 1, heads, rows, rows), F32), pltpu.VMEM((rows, 128), F32),
        pltpu.VMEM((heads, rows, PAIR), BF16), pltpu.VMEM((heads, rows, PAIR), BF16),
        pltpu.VMEM((heads, rows, PAIR), BF16), pltpu.VMEM((heads, rows, PAIR), BF16),
        pltpu.VMEM((width, rows), F32), pltpu.VMEM((2 * heads, rows), F32),
        pltpu.VMEM((width, rows), F32), pltpu.VMEM((width, rows), F32),
        pltpu.VMEM(block, F32), pltpu.VMEM(block, F32),
        pltpu.VMEM((pairs, rows, PAIR), BF16), pltpu.VMEM((rows + 2 * HALO, width), F32),
        pltpu.VMEM((8, rows + 2 * HALO, width), F32), pltpu.VMEM((8, rows + HALO, width), F32),
        pltpu.VMEM((rows + HALO + 8, width), F32),
        pltpu.VMEM((pairs, rows, PAIR), BF16),
        pltpu.VMEM((heads, rows, PAIR), BF16), pltpu.VMEM((heads, rows, PAIR), BF16),
        pltpu.VMEM((width, rows), F32), pltpu.VMEM((width, rows), F32),
        pltpu.VMEM(part_rows, BF16), pltpu.VMEM((pairs, 8, rows), F32),
        pltpu.VMEM(part_rows, BF16), pltpu.VMEM((pairs, 8, rows), F32),
        pltpu.VMEM(part_rows, BF16), pltpu.VMEM(part_rows, BF16),
    ] + relay_sems(near, (pairs,)) + relay_sems(reach) + relay_sems(reach, (pairs,)) + relay_sems(reach) + [
        pltpu.SemaphoreType.DMA((1 + 2 * pairs,)), pltpu.SemaphoreType.DMA((1 + 2 * pairs,)),
        pltpu.SemaphoreType.DMA((3,)), pltpu.SemaphoreType.DMA((3,)),
        pltpu.SemaphoreType.DMA((3 * pairs,)), pltpu.SemaphoreType.DMA((3 * pairs,)),
    ]
    vmem = pl.BlockSpec(memory_space=pltpu.VMEM)
    hbm = pl.BlockSpec(memory_space=pltpu.MemorySpace.HBM)
    results = pl.pallas_call(
        functools.partial(kernel, shards, reach, heads),
        out_shape=(pltpu.VMEM(block, BF16),) * 5,
        in_specs=[hbm] * 9,
        out_specs=(vmem,) * 5,
        scratch_shapes=scratch,
        compiler_params=pltpu.CompilerParams(
            collective_id=0, has_side_effects=True, vmem_limit_bytes=VMEM_BYTES),
    )(valid_counts, segment_ids, queries, keys, values, residual_in, out_proj,
      conv_kernel, cotangent)
    return pl.pallas_call(
        store_kernel,
        out_shape=(jax.ShapeDtypeStruct(block, BF16),) * 5,
        in_specs=[pl.BlockSpec(memory_space=pl.ANY)] * 5,
        out_specs=(hbm,) * 5,
        scratch_shapes=[pltpu.SemaphoreType.DMA((5,))],
    )(*[pltpu.with_memory_space_constraint(r, pltpu.VMEM) for r in results])


def solution(mesh):
    tokens = P(("groups", "tm"), "mp")
    in_specs = (tokens, tokens, tokens, tokens, P("mp", None), P(None, "mp"), P("groups"),
                P("groups"), tokens)
    return jax.shard_map(local, mesh=mesh, in_specs=in_specs, out_specs=(tokens,) * 5,
                         check_vma=False)
```

```python
import functools
import math

import jax
import jax.numpy as jnp
from jax import lax
from jax.experimental import pallas as pl
from jax.experimental.pallas import tpu as pltpu
from jax.sharding import PartitionSpec as P

HEAD_DIM = 64
PAIR = 2 * HEAD_DIM
HALO = 32
VMEM_BYTES = 63 * 1024 * 1024
LOG2E = math.log2(math.e)
MASKED = -1e30
MESH = pl.DeviceIdType.MESH
F32, BF16 = jnp.float32, jnp.bfloat16


def dot_nt(a, b):
    return lax.dot_general(a, b, (((1,), (1,)), ((), ())), preferred_element_type=F32)


def dot_nn(a, b):
    return jnp.dot(a, b, preferred_element_type=F32)


class Relay:
    def __init__(self, own, slot, recv, send_z, send_y, s, shards, reach, direction):
        self.own, self.slot, self.recv = own, slot, recv
        self.send_z, self.send_y = send_z, send_y
        self.s, self.shards, self.reach, self.direction = s, shards, reach, direction
        odd = lax.rem(s, 2)
        self.lead = odd == (0 if direction > 0 else 1)
        self.partner = s + 1 - 2 * odd
        self.target = s + 2 * direction
        self.has_target = (s + 2 < shards) if direction > 0 else (s >= 2)

    def exists(self, j):
        return (self.s - j >= 0) if self.direction > 0 else (self.s + j < self.shards)

    def source(self, j):
        return self.own if isinstance(j, int) and j == 0 else self.slot(j)

    def z_copy(self, j):
        return pltpu.make_async_remote_copy(
            src_ref=self.source(j), dst_ref=self.slot(j + 2),
            send_sem=self.send_z.at[j // 2], recv_sem=self.recv.at[j + 1],
            device_id={"tm": self.target}, device_id_type=MESH)

    def y_copy(self, j, landing):
        return pltpu.make_async_remote_copy(
            src_ref=self.source(j), dst_ref=self.slot(landing),
            send_sem=self.send_y.at[j // 2], recv_sem=self.recv.at[landing - 1],
            device_id={"tm": self.partner}, device_id_type=MESH)

    def each(self, j, act, along="zy"):
        at_start = isinstance(j, int) and j == 0
        here = self.exists(j)

        if "z" in along:
            @pl.when(here & self.has_target & (j <= self.reach - 2))
            def _():
                act(self.z_copy(j))

        if "y" not in along:
            return

        @pl.when(here & self.lead & (j <= self.reach - 2))
        def _():
            act(self.y_copy(j, j + 1))

        if not at_start:
            @pl.when(here & jnp.logical_not(self.lead))
            def _():
                act(self.y_copy(j, j - 1))

    def send(self, j, along="zy"):
        self.each(j, lambda copy: copy.start(), along)

    def forward(self, j, along="zy"):
        @pl.when(self.exists(j))
        def _():
            self.wait(j)
            self.send(j, along)

    def finish(self, j):
        @pl.when(j <= self.reach)
        def _():
            self.each(j, lambda copy: copy.wait_send())

    def wait(self, j):
        pltpu.make_async_remote_copy(
            src_ref=self.slot(j), dst_ref=self.slot(j),
            send_sem=self.send_z.at[0], recv_sem=self.recv.at[j - 1],
            device_id={"tm": self.partner}, device_id_type=MESH).wait_recv()


def kernel(shards, reach, heads,
           counts_in, seg_in, q_in, k_in, v_in, res_in, w_in, taps_in, cot_in,
           out_ref, gin_ref, gq_ref, gk_ref, gv_ref,
           q_ref, kv_ref, res_ref, w_ref, taps_ref, cot_ref, counts_ref, seg_ref, load_sem, kv_sem, seg_sem,
           kvbuf, qbuf, abuf, sbuf, woth, aown, aoth, goth,
           hid, prev, nxt, cnext,
           bias, kept, colown, qm, km, vm, am, otr, stats, atr, dqt, dkacc, dvacc,
           da, ext, shifted, spread, gconv, gown,
           qfar, afar, ofar, dfar, part_out, part_stats, far_out, far_stats, part_dq, far_dq,
           kvrecv, kvz, kvy, qrecv, qz, qy, arecv, az, ay, srecv, sz, sy,
           pair_send, pair_recv, halo_send, halo_recv, far_send, far_recv):
    rows, width = q_ref.shape
    pairs = width // PAIR
    kv_loads = [pltpu.make_async_copy(src.at[:, g * PAIR:(g + 1) * PAIR], kv_ref.at[g, index],
                                      kv_sem.at[g, index])
                for g in range(pairs) for index, src in enumerate((k_in, v_in))]
    loads = [pltpu.make_async_copy(src, dst, load_sem.at[index])
             for index, (src, dst) in enumerate((
                 (q_in, q_ref), (res_in, res_ref), (w_in, w_ref),
                 (taps_in, taps_ref), (cot_in, cot_ref), (counts_in, counts_ref)))]
    seg_loads = [pltpu.make_async_copy(seg_in.at[pl.ds(shard * rows, rows)], seg_ref.at[shard],
                                       seg_sem) for shard in range(shards)]
    for load in kv_loads + loads + seg_loads:
        load.start()
    s = lax.axis_index("tm")
    mp = lax.axis_index("mp")
    other = 1 - mp
    odd = lax.rem(s, 2)
    scale = HEAD_DIM ** -0.5
    to_log2 = scale * LOG2E

    barrier = pltpu.get_barrier_semaphore()
    for shift in (-2, -1, 1, 2):
        @pl.when((s + shift >= 0) & (s + shift < shards))
        def _():
            pl.semaphore_signal(barrier, inc=1, device_id={"tm": s + shift}, device_id_type=MESH)
    pl.semaphore_signal(barrier, inc=1, device_id={"mp": other}, device_id_type=MESH)
    peers = jnp.minimum(s, 2) + jnp.minimum(shards - 1 - s, 2) + 1
    pl.semaphore_wait(barrier, peers)

    near = reach - 2

    def part_relays(own, buf, sems, span, direction):
        return [Relay(own.at[g], lambda j, g=g: buf.at[g, j - 1], *(sem.at[g] for sem in sems),
                      s, shards, span, direction) for g in range(pairs)]

    kv_up = part_relays(kv_ref, kvbuf, (kvrecv, kvz, kvy), near, 1)
    q_down = Relay(q_in, lambda j: qbuf.at[j - 1], qrecv, qz, qy, s, shards, reach, -1)
    a_down = part_relays(da, abuf, (arecv, az, ay), reach, -1)
    s_down = Relay(stats, lambda j: sbuf.at[j - 1], srecv, sz, sy, s, shards, reach, -1)

    for load in kv_loads:
        load.wait()
    for g in range(pairs):
        kv_up[g].send(0)
        if g == 0:
            q_down.send(0, "z")

    helps = (s + 2 < shards) & (s >= reach - 3)
    helped = s >= reach - 1

    def far_copy(index, src, dst):
        return pltpu.make_async_remote_copy(
            src_ref=src, dst_ref=dst, send_sem=far_send.at[index], recv_sem=far_recv.at[index],
            device_id={"tm": s + 2}, device_id_type=MESH)

    def far_copies(g):
        return (far_copy(3 * g, part_out.at[g], far_out.at[g]),
                far_copy(3 * g + 1, part_stats.at[g], far_stats.at[g]))

    def far_grad_copy(g):
        return far_copy(3 * g + 2, part_dq.at[g], far_dq.at[g])

    def pair_copy(index, src, dst):
        return pltpu.make_async_remote_copy(
            src_ref=src, dst_ref=dst, send_sem=pair_send.at[index], recv_sem=pair_recv.at[index],
            device_id={"mp": other}, device_id_type=MESH)

    own_cols = pl.ds(pl.multiple_of(mp * width, width), width)
    other_cols = pl.ds(pl.multiple_of(other * width, width), width)
    w_copy = pair_copy(0, w_in.at[:, other_cols], woth)
    w_copy.start()

    def halo_copy(index, src, dst, shift):
        return pltpu.make_async_remote_copy(
            src_ref=src, dst_ref=dst, send_sem=halo_send.at[index], recv_sem=halo_recv.at[index],
            device_id={"tm": s + shift}, device_id_type=MESH)

    has_prev, has_next = s > 0, s < shards - 1
    cot_copy = halo_copy(0, cot_in.at[pl.ds(0, HALO)], cnext, -1)
    last_copy = halo_copy(1, hid.at[pl.ds(rows - HALO, HALO)], prev, 1)
    first_copy = halo_copy(2, hid.at[pl.ds(0, HALO)], nxt, -1)

    @pl.when(has_prev)
    def _():
        cot_copy.start()

    @pl.when(jnp.logical_not(has_prev))
    def _():
        prev[...] = jnp.zeros_like(prev)

    @pl.when(jnp.logical_not(has_next))
    def _():
        nxt[...] = jnp.zeros_like(nxt)
        cnext[...] = jnp.zeros_like(cnext)

    for load in loads:
        load.wait()
    pltpu.make_async_copy(seg_ref, seg_ref, seg_sem).wait()

    lane = lax.broadcasted_iota(jnp.int32, (rows, PAIR), 1)
    low = lane < HEAD_DIM

    def only(block, h):
        keep = low if h % 2 == 0 else jnp.logical_not(low)
        return jnp.where(keep, block.astype(F32), 0.0).astype(BF16)

    def cols(g):
        return slice(g * PAIR, (g + 1) * PAIR)

    def head_rows(h):
        return slice(h * HEAD_DIM, (h + 1) * HEAD_DIM)

    for h in range(heads):
        qm[h] = only(q_ref[:, cols(h // 2)], h)
        km[h] = only(kv_ref[h // 2, 0], h)
        vm[h] = only(kv_ref[h // 2, 1], h)

    def seg_row(shard):
        return seg_ref[pl.ds(shard, 1), :]

    def label_col(shard):
        position = lax.broadcasted_iota(jnp.int32, (1, rows), 1)
        label = jnp.where(position < counts_ref[shard], seg_row(shard), -1).astype(F32)
        return jnp.broadcast_to(label, (128, rows)).T

    own_seg = seg_row(s).astype(F32)

    def fill_bias(slot, col, segs, diagonal):
        for part in range(rows // 128):
            at = slice(part * 128, (part + 1) * 128)
            seen = col == segs[:, at]
            if diagonal:
                key_at = lax.broadcasted_iota(jnp.int32, (rows, 128), 0)
                query_at = lax.broadcasted_iota(jnp.int32, (rows, 128), 1) + part * 128
                seen = (seen & (key_at < query_at)) | (key_at == query_at)
            bias[slot, :, at] = jnp.where(seen, 0.0, MASKED)

    colown[...] = label_col(s)
    fill_bias(0, colown[...], own_seg, True)

    def forward_pair(g, kblk, vblk, targets):
        vtr = vblk.astype(F32).T.astype(BF16)
        for slot, masked_q, totals, out, first in targets:
            for h in (2 * g, 2 * g + 1):
                at_top, at_mass = totals(h)
                scores = dot_nt(kblk, masked_q[h]) * to_log2 + bias[slot]
                kept[slot, h] = scores
                top = jnp.max(scores, axis=0, keepdims=True)
                if not first:
                    top = jnp.maximum(at_top[...], top)
                weights = jnp.exp2(scores - top)
                mass = jnp.sum(weights, axis=0, keepdims=True)
                part = dot_nn(vtr[head_rows(h - 2 * g)], weights.astype(BF16))
                if not first:
                    fade = jnp.exp2(at_top[...] - top)
                    mass = mass + at_mass[...] * fade
                    part = part + out[head_rows(h), :] * fade
                at_top[...] = top
                at_mass[...] = mass
                out[head_rows(h), :] = part

    def own_totals(h):
        return stats.at[h:h + 1, :], stats.at[heads + h:heads + h + 1, :]

    def far_totals(h):
        g, at = h // 2, h % 2
        return part_stats.at[g, at:at + 1, :], part_stats.at[g, 2 + at:3 + at, :]

    def own_target(slot, first=False):
        return slot, qm, own_totals, otr, first

    def far_target(slot):
        return slot, qfar, far_totals, ofar, False

    for g in range(pairs):
        forward_pair(g, kv_ref[g, 0], kv_ref[g, 1], [own_target(0, True)])
        part_stats[g, 0:2, :] = jnp.full((2, rows), 2 * MASKED, F32)
        part_stats[g, 2:, :] = jnp.zeros((6, rows), F32)
    ofar[...] = jnp.zeros_like(ofar)

    def own_step(i):
        return jnp.where(odd == 1, i, jnp.where(lax.rem(i, 2) == 1, i + 1, i - 1))

    if near > 2:
        @pl.loop(1, near - 1)
        def _(i):
            j = own_step(i)

            @pl.when(s - j >= 0)
            def _():
                fill_bias(j, label_col(s - j), own_seg, False)

            for g in range(pairs):
                @pl.when(lax.rem(i, 2) == 1)
                def _():
                    kv_up[g].forward(i + 1)

                @pl.when(s - j >= 0)
                def _():
                    @pl.when(lax.rem(j, 2) == 1)
                    def _():
                        kv_up[g].wait(j)

                    forward_pair(g, kvbuf[g, j - 1, 0], kvbuf[g, j - 1, 1], [own_target(j)])

    for d in (near - 1, near):
        @pl.when(s - d >= 0)
        def _():
            col = label_col(s - d)
            fill_bias(d, col, own_seg, False)
            fill_bias(d + 2, col, seg_row(jnp.minimum(s + 2, shards - 1)).astype(F32), False)

    q_down.forward(2, "z")
    for j in range(1, reach + 1):
        @pl.when(s + j < shards)
        def _():
            fill_bias(reach + j, colown[...], seg_row(s + j).astype(F32), False)

    for g in range(pairs):
        @pl.when(helps)
        def _():
            for h in (2 * g, 2 * g + 1):
                qfar[h] = only(qbuf[1, :, cols(g)], h)

        kv_up[g].forward(near)
        j = own_step(near - 1)

        @pl.when(s - j >= 0)
        def _():
                @pl.when(lax.rem(j, 2) == 1)
                def _():
                    kv_up[g].wait(j)

                forward_pair(g, kvbuf[g, j - 1, 0], kvbuf[g, j - 1, 1], [far_target(j + 2), own_target(j)])

        last_j = own_step(near)

        @pl.when(s - last_j >= 0)
        def _():
                @pl.when(lax.rem(last_j, 2) == 1)
                def _():
                    kv_up[g].wait(last_j)

                forward_pair(g, kvbuf[g, last_j - 1, 0], kvbuf[g, last_j - 1, 1], [far_target(last_j + 2)])

        @pl.when(helps)
        def _():
            part_out[g] = ofar[cols(g), :].astype(BF16)
            for copy in far_copies(g):
                copy.start()

        @pl.when(s - last_j >= 0)
        def _():
            forward_pair(g, kvbuf[g, last_j - 1, 0], kvbuf[g, last_j - 1, 1], [own_target(last_j)])

    for g in range(pairs):
        @pl.when(helped)
        def _():
            for copy in far_copies(g):
                copy.wait_recv()
            for at in (0, 1):
                h = 2 * g + at
                at_top, at_mass = own_totals(h)
                far_top = far_stats[g, at:at + 1, :]
                top = jnp.maximum(at_top[...], far_top)
                fade, far_fade = jnp.exp2(at_top[...] - top), jnp.exp2(far_top - top)
                at_top[...] = top
                at_mass[...] = at_mass[...] * fade + far_stats[g, 2 + at:3 + at, :] * far_fade
                far_part = far_out[g, head_rows(at), :].astype(F32)
                otr[head_rows(h), :] = otr[head_rows(h), :] * fade + far_part * far_fade

        for h in (2 * g, 2 * g + 1):
            atr[head_rows(h), :] = otr[head_rows(h), :] / stats[heads + h:heads + h + 1, :]
        block = atr[cols(g), :]
        aown[g] = block.T.astype(BF16)
        atr[cols(g), :] = block.astype(BF16).astype(F32)
        pair_copy(1 + g, aown.at[g], aoth.at[g]).start()
    for h in range(heads):
        stats[h:h + 1, :] = stats[h:h + 1, :] + jnp.log(stats[heads + h:heads + h + 1, :]) * LOG2E

    mixed = res_ref[...].astype(F32)
    w_own = w_ref[:, own_cols]
    for g in range(pairs):
        mixed = mixed + dot_nn(aown[g], w_own[cols(g), :])
    w_copy.wait_recv()
    for g in range(pairs):
        pair_copy(1 + g, aown.at[g], aoth.at[g]).wait_recv()
        mixed = mixed + dot_nn(aoth[g], woth[cols(g), :])
    hid[...] = mixed.astype(BF16)

    @pl.when(has_next)
    def _():
        last_copy.start()

    @pl.when(has_prev)
    def _():
        first_copy.start()

    q_down.send(0, "y")
    q_down.send(2, "y")

    @pl.loop(2, reach // 2 + 1)
    def _(i):
        q_down.forward(2 * i)

    long = rows + HALO
    tap_count = taps_ref.shape[0]
    taps = taps_ref[...].astype(F32)

    def shift_hidden(start, stop):
        for r in range(8):
            shifted[r, start:stop, :] = ext[start - r:stop - r, :]

    def shift_grad(start, stop):
        for r in range(8):
            spread[r, start:stop, :] = gconv[start + r:stop + r, :]

    def convolve(g, start, stop):
        size = stop - start
        mix = jnp.zeros((size, PAIR), F32)
        for tap in range(tap_count):
            at = HALO + start - 8 * (tap // 8)
            mix = mix + taps[tap:tap + 1, cols(g)] * shifted[tap % 8, at:at + size, cols(g)]
        gate = jax.nn.sigmoid(mix)
        if start < rows:
            up = cot_ref[start:stop, cols(g)].astype(F32)
            hidden = ext[HALO + start:HALO + stop, cols(g)]
            out_ref[start:stop, cols(g)] = (hidden + mix * gate).astype(BF16)
        else:
            up = cnext[:, cols(g)].astype(F32)
        gconv[start:stop, cols(g)] = up * gate * (1.0 + mix * (1.0 - gate))

    def convolve_back(g, start, stop):
        grad = cot_ref[start:stop, cols(g)].astype(F32)
        for tap in range(tap_count):
            at = start + 8 * (tap // 8)
            grad = grad + taps[tap:tap + 1, cols(g)] * spread[tap % 8, at:at + stop - start, cols(g)]
        gown[g, start:stop, :] = grad.astype(BF16)

    ext[HALO:HALO + rows, :] = hid[...].astype(F32)
    gconv[long:, :] = jnp.zeros((8, width), F32)
    shift_hidden(HALO + 8, HALO + rows)
    step, back_step = (rows - HALO) // 2, (rows - 2 * HALO) // 2
    for g in range(pairs):
        for start in range(HALO, rows, step):
            convolve(g, start, start + step)
    shift_grad(HALO, rows - 8)
    for g in range(pairs):
        for start in range(HALO, rows - HALO, back_step):
            convolve_back(g, start, start + back_step)

    @pl.when(has_next)
    def _():
        first_copy.wait_recv()
        cot_copy.wait_recv()

    @pl.when(has_prev)
    def _():
        last_copy.wait_recv()

    ext[0:HALO, :] = prev[...].astype(F32)
    ext[HALO + rows:, :] = nxt[...].astype(F32)
    shift_hidden(8, HALO + 8)
    shift_hidden(HALO + rows, long + HALO)
    for g in range(pairs):
        convolve(g, 0, HALO)
        convolve(g, rows, long)
    shift_grad(0, HALO)
    shift_grad(rows - 8, long)
    for g in range(pairs):
        convolve_back(g, 0, HALO)
        convolve_back(g, rows - HALO, rows)
        gin_ref[:, cols(g)] = gown[g]
        pair_copy(1 + pairs + g, gown.at[g], goth.at[g]).start()

    w_mine = [w_ref[:, pl.ds(pl.multiple_of(mp * width + g * PAIR, PAIR), PAIR)] for g in range(pairs)]
    w_far = [w_ref[:, pl.ds(pl.multiple_of(other * width + g * PAIR, PAIR), PAIR)] for g in range(pairs)]
    grad = dot_nt(gown[0], w_mine[0])
    gradt = dot_nt(w_mine[0], gown[0])
    for g in range(1, pairs):
        grad = grad + dot_nt(gown[g], w_mine[g])
        gradt = gradt + dot_nt(w_mine[g], gown[g])
    for g in range(pairs):
        pair_copy(1 + pairs + g, gown.at[g], goth.at[g]).wait_recv()
        grad = grad + dot_nt(goth[g], w_far[g])
        gradt = gradt + dot_nt(w_far[g], goth[g])
    for g in range(pairs):
        da[g] = grad[:, cols(g)].astype(BF16)
    products = gradt.astype(BF16).astype(F32) * atr[...]
    for h in range(heads):
        stats[heads + h:heads + h + 1, :] = jnp.sum(products[head_rows(h)], axis=0, keepdims=True)
    s_down.send(0)
    for g in range(pairs):
        a_down[g].send(0)
    for h in range(heads):
        am[h] = only(da[h // 2], h)

    def query_pair(slot, g, kblk, vblk, masked_a, tops, dots, grad_q, first, own=False):
        ktr = kblk.astype(F32).T.astype(BF16)
        sums = []
        for h in (2 * g, 2 * g + 1):
            weights = jnp.exp2(kept[slot, h] - tops(h))
            pushes = dot_nt(vblk, masked_a[h])
            slopes = (weights * (pushes - dots(h))).astype(BF16)
            part = dot_nn(ktr[head_rows(h - 2 * g)], slopes)
            grad_q[head_rows(h), :] = part if first else grad_q[head_rows(h), :] + part
            if own:
                sums.append((dot_nn(slopes, q_ref[:, cols(g)]),
                             dot_nn(weights.astype(BF16), da[g])))
        if own:
            dkacc[:, cols(g)] = jnp.where(low, sums[0][0], sums[1][0])
            dvacc[:, cols(g)] = jnp.where(low, sums[0][1], sums[1][1])

    own_rows = (lambda h: stats[h:h + 1, :], lambda h: stats[heads + h:heads + h + 1, :])
    far_rows = (lambda h: sbuf[1, h:h + 1, :], lambda h: sbuf[1, heads + h:heads + h + 1, :])

    for g in range(pairs):
        query_pair(0, g, kv_ref[g, 0], kv_ref[g, 1], am, *own_rows, dqt, True, True)

    def own_queries(i):
        @pl.when(s - i >= 0)
        def _():
            for g in range(pairs):
                query_pair(i, g, kvbuf[g, i - 1, 0], kvbuf[g, i - 1, 1], am, *own_rows, dqt, False)

    def key_pair(j, g):
        qblk, ablk, far = qbuf[j - 1, :, cols(g)], abuf[g, j - 1], sbuf[j - 1]
        sums = []
        for h in (2 * g, 2 * g + 1):
            scores = dot_nt(km[h], qblk) * to_log2 + bias[reach + j]
            weights = jnp.exp2(scores - far[h:h + 1, :])
            pushes = dot_nt(vm[h], ablk)
            slopes = (weights * (pushes - far[heads + h:heads + h + 1, :])).astype(BF16)
            sums.append((dot_nn(slopes, qblk), dot_nn(weights.astype(BF16), ablk)))
        dkacc[:, cols(g)] = dkacc[:, cols(g)] + jnp.where(low, sums[0][0], sums[1][0])
        dvacc[:, cols(g)] = dvacc[:, cols(g)] + jnp.where(low, sums[0][1], sums[1][1])

    def forward_grad(j):
        s_down.forward(j)
        for g in range(pairs):
            a_down[g].forward(j)

    def keys_even(j):
        @pl.when(s + j < shards)
        def _():
            for g in range(pairs):
                key_pair(j, g)

    def keys_odd(j):
        @pl.when(s + j < shards)
        def _():
            s_down.wait(j)
            q_down.wait(j)
            for g in range(pairs):
                a_down[g].wait(j)
                key_pair(j, g)

    def far_grads(both, parts):
        for g in parts:
            for h in (2 * g, 2 * g + 1):
                afar[h] = only(abuf[g, 1], h)
            for d in (near - 1, near)[:2 if both else 1]:
                query_pair(d + 2, g, kvbuf[g, d - 1, 0], kvbuf[g, d - 1, 1], afar, *far_rows, dfar, d < near)
            part_dq[g] = dfar[cols(g), :].astype(BF16)
            far_grad_copy(g).start()

    if near == 2:
        own_queries(1)
        own_queries(2)
    else:
        pl.loop(1, near + 1)(own_queries)

    def far_step(parity, parts):
        @pl.when(helps & (odd == parity) & (s >= near))
        def _():
            far_grads(True, parts)

        if (near - 1) % 2 == parity:
            @pl.when(helps & (s == near - 1))
            def _():
                far_grads(False, parts)

    forward_grad(2)
    far_step(1, range(pairs))
    keys_even(2)
    keys_odd(1)
    far_step(0, range(1))
    forward_grad(4)
    far_step(0, range(1, pairs))
    keys_even(4)
    def finish_queries():
        @pl.when(helped)
        def _():
            for g in range(pairs):
                far_grad_copy(g).wait_recv()
                dqt[cols(g), :] = dqt[cols(g), :] + far_dq[g].astype(F32)

        gq_ref[...] = (dqt[...] * scale).T.astype(BF16)

    @pl.when(s < reach)
    def _():
        finish_queries()

    keys_odd(3)

    if reach > 4:
        @pl.loop(3, reach // 2 + 1)
        def _(i):
            forward_grad(2 * i)
            keys_even(2 * i)
            keys_odd(2 * i - 1)

    @pl.when(s >= reach)
    def _():
        finish_queries()

    gk_ref[...] = (dkacc[...] * scale).astype(BF16)
    gv_ref[...] = dvacc[...].astype(BF16)

    flat = (*kv_up, q_down, *a_down, s_down)
    for relay in flat:
        relay.finish(0)

    @pl.loop(1, reach // 2 + 1)
    def _(i):
        for relay in flat:
            relay.finish(2 * i)

    @pl.when(helps)
    def _():
        for g in range(pairs):
            for copy in (*far_copies(g), far_grad_copy(g)):
                copy.wait_send()

    w_copy.wait_send()
    for g in range(pairs):
        pair_copy(1 + g, aown.at[g], aoth.at[g]).wait_send()
        pair_copy(1 + pairs + g, gown.at[g], goth.at[g]).wait_send()

    @pl.when(has_prev)
    def _():
        cot_copy.wait_send()
        first_copy.wait_send()

    @pl.when(has_next)
    def _():
        last_copy.wait_send()


def store_kernel(*refs):
    count = len(refs) // 2
    stores = [pltpu.make_async_copy(refs[index], refs[count + index], refs[-1].at[index])
              for index in range(count)]
    for store in stores:
        store.start()
    for store in stores:
        store.wait()


def local(queries, keys, values, residual_in, out_proj, conv_kernel, valid_counts, segment_ids,
          cotangent):
    rows, width = queries.shape
    heads = width // HEAD_DIM
    pairs = width // PAIR
    shards = valid_counts.shape[0]
    window = segment_ids.shape[0]
    reach = -(-(window // 2) // rows)
    block = (rows, width)
    sems = pltpu.SemaphoreType.DMA
    near = reach - 2
    part_rows = (pairs, PAIR, rows)

    def relay_sems(span, parts=()):
        return [sems(parts + (span,)), sems(parts + (span // 2 + 1,)), sems(parts + (span // 2 + 1,))]

    scratch = [pltpu.VMEM(block, BF16), pltpu.VMEM((pairs, 2, rows, PAIR), BF16),
               pltpu.VMEM(block, BF16)] + [
        pltpu.VMEM(out_proj.shape, BF16), pltpu.VMEM(conv_kernel.shape, BF16),
        pltpu.VMEM(block, BF16), pltpu.SMEM(valid_counts.shape, jnp.int32),
        pltpu.VMEM((shards, rows), jnp.int32),
        pltpu.SemaphoreType.DMA((6,)), pltpu.SemaphoreType.DMA((pairs, 2)), pltpu.SemaphoreType.DMA,
        pltpu.VMEM((pairs, near, 2, rows, PAIR), BF16),
        pltpu.VMEM((reach,) + block, BF16), pltpu.VMEM((pairs, reach, rows, PAIR), BF16),
        pltpu.VMEM((reach, 2 * heads, rows), F32),
        pltpu.VMEM(block, BF16),
        pltpu.VMEM((pairs, rows, PAIR), BF16), pltpu.VMEM((pairs, rows, PAIR), BF16),
        pltpu.VMEM((pairs, rows, PAIR), BF16),
        pltpu.VMEM(block, BF16), pltpu.VMEM((HALO, width), BF16), pltpu.VMEM((HALO, width), BF16),
        pltpu.VMEM((HALO, width), BF16),
        pltpu.VMEM((2 * reach + 1, rows, rows), F32), pltpu.VMEM((reach + 1, heads, rows, rows), F32), pltpu.VMEM((rows, 128), F32),
        pltpu.VMEM((heads, rows, PAIR), BF16), pltpu.VMEM((heads, rows, PAIR), BF16),
        pltpu.VMEM((heads, rows, PAIR), BF16), pltpu.VMEM((heads, rows, PAIR), BF16),
        pltpu.VMEM((width, rows), F32), pltpu.VMEM((2 * heads, rows), F32),
        pltpu.VMEM((width, rows), F32), pltpu.VMEM((width, rows), F32),
        pltpu.VMEM(block, F32), pltpu.VMEM(block, F32),
        pltpu.VMEM((pairs, rows, PAIR), BF16), pltpu.VMEM((rows + 2 * HALO, width), F32),
        pltpu.VMEM((8, rows + 2 * HALO, width), F32), pltpu.VMEM((8, rows + HALO, width), F32),
        pltpu.VMEM((rows + HALO + 8, width), F32),
        pltpu.VMEM((pairs, rows, PAIR), BF16),
        pltpu.VMEM((heads, rows, PAIR), BF16), pltpu.VMEM((heads, rows, PAIR), BF16),
        pltpu.VMEM((width, rows), F32), pltpu.VMEM((width, rows), F32),
        pltpu.VMEM(part_rows, BF16), pltpu.VMEM((pairs, 8, rows), F32),
        pltpu.VMEM(part_rows, BF16), pltpu.VMEM((pairs, 8, rows), F32),
        pltpu.VMEM(part_rows, BF16), pltpu.VMEM(part_rows, BF16),
    ] + relay_sems(near, (pairs,)) + relay_sems(reach) + relay_sems(reach, (pairs,)) + relay_sems(reach) + [
        pltpu.SemaphoreType.DMA((1 + 2 * pairs,)), pltpu.SemaphoreType.DMA((1 + 2 * pairs,)),
        pltpu.SemaphoreType.DMA((3,)), pltpu.SemaphoreType.DMA((3,)),
        pltpu.SemaphoreType.DMA((3 * pairs,)), pltpu.SemaphoreType.DMA((3 * pairs,)),
    ]
    vmem = pl.BlockSpec(memory_space=pltpu.VMEM)
    hbm = pl.BlockSpec(memory_space=pltpu.MemorySpace.HBM)
    results = pl.pallas_call(
        functools.partial(kernel, shards, reach, heads),
        out_shape=(pltpu.VMEM(block, BF16),) * 5,
        in_specs=[hbm] * 9,
        out_specs=(vmem,) * 5,
        scratch_shapes=scratch,
        compiler_params=pltpu.CompilerParams(
            collective_id=0, has_side_effects=True, vmem_limit_bytes=VMEM_BYTES),
    )(valid_counts, segment_ids, queries, keys, values, residual_in, out_proj,
      conv_kernel, cotangent)
    return pl.pallas_call(
        store_kernel,
        out_shape=(jax.ShapeDtypeStruct(block, BF16),) * 5,
        in_specs=[pl.BlockSpec(memory_space=pl.ANY)] * 5,
        out_specs=(hbm,) * 5,
        scratch_shapes=[pltpu.SemaphoreType.DMA((5,))],
    )(*[pltpu.with_memory_space_constraint(r, pltpu.VMEM) for r in results])


def solution(mesh):
    tokens = P(("groups", "tm"), "mp")
    in_specs = (tokens, tokens, tokens, tokens, P("mp", None), P(None, "mp"), P("groups"),
                P("groups"), tokens)
    return jax.shard_map(local, mesh=mesh, in_specs=in_specs, out_specs=(tokens,) * 5,
                         check_vma=False)
```

```python
import functools
import math

import jax
import jax.numpy as jnp
from jax import lax
from jax.experimental import pallas as pl
from jax.experimental.pallas import tpu as pltpu
from jax.sharding import PartitionSpec as P

HEAD_DIM = 64
PAIR = 2 * HEAD_DIM
HALO = 32
VMEM_BYTES = 63 * 1024 * 1024
LOG2E = math.log2(math.e)
MASKED = -1e30
MESH = pl.DeviceIdType.MESH
F32, BF16 = jnp.float32, jnp.bfloat16


def dot_nt(a, b):
    return lax.dot_general(a, b, (((1,), (1,)), ((), ())), preferred_element_type=F32)


def dot_nn(a, b):
    return jnp.dot(a, b, preferred_element_type=F32)


class Relay:
    def __init__(self, own, slot, recv, send_z, send_y, s, shards, reach, direction):
        self.own, self.slot, self.recv = own, slot, recv
        self.send_z, self.send_y = send_z, send_y
        self.s, self.shards, self.reach, self.direction = s, shards, reach, direction
        odd = lax.rem(s, 2)
        self.lead = odd == (0 if direction > 0 else 1)
        self.partner = s + 1 - 2 * odd
        self.target = s + 2 * direction
        self.has_target = (s + 2 < shards) if direction > 0 else (s >= 2)

    def exists(self, j):
        return (self.s - j >= 0) if self.direction > 0 else (self.s + j < self.shards)

    def source(self, j):
        return self.own if isinstance(j, int) and j == 0 else self.slot(j)

    def z_copy(self, j):
        return pltpu.make_async_remote_copy(
            src_ref=self.source(j), dst_ref=self.slot(j + 2),
            send_sem=self.send_z.at[j // 2], recv_sem=self.recv.at[j + 1],
            device_id={"tm": self.target}, device_id_type=MESH)

    def y_copy(self, j, landing):
        return pltpu.make_async_remote_copy(
            src_ref=self.source(j), dst_ref=self.slot(landing),
            send_sem=self.send_y.at[j // 2], recv_sem=self.recv.at[landing - 1],
            device_id={"tm": self.partner}, device_id_type=MESH)

    def each(self, j, act, along="zy"):
        at_start = isinstance(j, int) and j == 0
        here = self.exists(j)

        if "z" in along:
            @pl.when(here & self.has_target & (j <= self.reach - 2))
            def _():
                act(self.z_copy(j))

        if "y" not in along:
            return

        @pl.when(here & self.lead & (j <= self.reach - 2))
        def _():
            act(self.y_copy(j, j + 1))

        if not at_start:
            @pl.when(here & jnp.logical_not(self.lead))
            def _():
                act(self.y_copy(j, j - 1))

    def send(self, j, along="zy"):
        self.each(j, lambda copy: copy.start(), along)

    def forward(self, j, along="zy"):
        @pl.when(self.exists(j))
        def _():
            self.wait(j)
            self.send(j, along)

    def finish(self, j):
        @pl.when(j <= self.reach)
        def _():
            self.each(j, lambda copy: copy.wait_send())

    def wait(self, j):
        pltpu.make_async_remote_copy(
            src_ref=self.slot(j), dst_ref=self.slot(j),
            send_sem=self.send_z.at[0], recv_sem=self.recv.at[j - 1],
            device_id={"tm": self.partner}, device_id_type=MESH).wait_recv()


def kernel(shards, reach, heads,
           counts_in, seg_in, q_in, k_in, v_in, res_in, w_in, taps_in, cot_in,
           out_ref, gin_ref, gq_ref, gk_ref, gv_ref,
           q_ref, kv_ref, res_ref, w_ref, taps_ref, cot_ref, counts_ref, seg_ref, load_sem, kv_sem, seg_sem,
           kvbuf, qbuf, abuf, sbuf, woth, aown, aoth, goth,
           hid, prev, nxt, cnext,
           bias, kept, colown, qm, km, vm, am, otr, stats, atr, dqt, dkacc, dvacc,
           da, ext, shifted, spread, gconv, gown,
           qfar, afar, ofar, dfar, part_out, part_stats, far_out, far_stats, part_dq, far_dq,
           ahead,
           kvrecv, kvz, kvy, qrecv, qz, qy, arecv, az, ay, srecv, sz, sy,
           pair_send, pair_recv, halo_send, halo_recv, far_send, far_recv):
    rows, width = q_ref.shape
    pairs = width // PAIR
    kv_loads = [pltpu.make_async_copy(src.at[:, g * PAIR:(g + 1) * PAIR], kv_ref.at[g, index],
                                      kv_sem.at[g, index])
                for g in range(pairs) for index, src in enumerate((k_in, v_in))]
    loads = [pltpu.make_async_copy(src, dst, load_sem.at[index])
             for index, (src, dst) in enumerate((
                 (q_in, q_ref), (res_in, res_ref), (w_in, w_ref),
                 (taps_in, taps_ref), (cot_in, cot_ref), (counts_in, counts_ref)))]
    seg_loads = [pltpu.make_async_copy(seg_in.at[pl.ds(shard * rows, rows)], seg_ref.at[shard],
                                       seg_sem) for shard in range(shards)]
    for load in kv_loads + loads + seg_loads:
        load.start()
    s = lax.axis_index("tm")
    mp = lax.axis_index("mp")
    other = 1 - mp
    odd = lax.rem(s, 2)
    scale = HEAD_DIM ** -0.5
    to_log2 = scale * LOG2E

    barrier = pltpu.get_barrier_semaphore()
    for shift in (-2, -1, 1, 2):
        @pl.when((s + shift >= 0) & (s + shift < shards))
        def _():
            pl.semaphore_signal(barrier, inc=1, device_id={"tm": s + shift}, device_id_type=MESH)
    pl.semaphore_signal(barrier, inc=1, device_id={"mp": other}, device_id_type=MESH)
    peers = jnp.minimum(s, 2) + jnp.minimum(shards - 1 - s, 2) + 1
    pl.semaphore_wait(barrier, peers)

    near = reach - 2

    def part_relays(own, buf, sems, span, direction):
        return [Relay(own.at[g], lambda j, g=g: buf.at[g, j - 1], *(sem.at[g] for sem in sems),
                      s, shards, span, direction) for g in range(pairs)]

    kv_up = part_relays(kv_ref, kvbuf, (kvrecv, kvz, kvy), near, 1)
    q_down = Relay(q_in, lambda j: qbuf.at[j - 1], qrecv, qz, qy, s, shards, reach, -1)
    a_down = part_relays(da, abuf, (arecv, az, ay), reach, -1)
    s_down = Relay(stats, lambda j: sbuf.at[j - 1], srecv, sz, sy, s, shards, reach, -1)

    for load in kv_loads:
        load.wait()
    for g in range(pairs):
        kv_up[g].send(0)
        if g == 0:
            q_down.send(0, "z")

    helps = (s + 2 < shards) & (s >= reach - 3)
    helped = s >= reach - 1

    def far_copy(index, src, dst):
        return pltpu.make_async_remote_copy(
            src_ref=src, dst_ref=dst, send_sem=far_send.at[index], recv_sem=far_recv.at[index],
            device_id={"tm": s + 2}, device_id_type=MESH)

    def far_copies(g):
        return (far_copy(3 * g, part_out.at[g], far_out.at[g]),
                far_copy(3 * g + 1, part_stats.at[g], far_stats.at[g]))

    def far_grad_copy(g):
        return far_copy(3 * g + 2, part_dq.at[g], far_dq.at[g])

    def pair_copy(index, src, dst):
        return pltpu.make_async_remote_copy(
            src_ref=src, dst_ref=dst, send_sem=pair_send.at[index], recv_sem=pair_recv.at[index],
            device_id={"mp": other}, device_id_type=MESH)

    own_cols = pl.ds(pl.multiple_of(mp * width, width), width)
    other_cols = pl.ds(pl.multiple_of(other * width, width), width)
    w_copy = pair_copy(0, w_in.at[:, other_cols], woth)
    w_copy.start()

    def halo_copy(index, src, dst, shift):
        return pltpu.make_async_remote_copy(
            src_ref=src, dst_ref=dst, send_sem=halo_send.at[index], recv_sem=halo_recv.at[index],
            device_id={"tm": s + shift}, device_id_type=MESH)

    has_prev, has_next = s > 0, s < shards - 1
    cot_copy = halo_copy(0, cot_in.at[pl.ds(0, HALO)], cnext, -1)
    last_copy = halo_copy(1, hid.at[pl.ds(rows - HALO, HALO)], prev, 1)
    first_copy = halo_copy(2, hid.at[pl.ds(0, HALO)], nxt, -1)

    @pl.when(has_prev)
    def _():
        cot_copy.start()

    @pl.when(jnp.logical_not(has_prev))
    def _():
        prev[...] = jnp.zeros_like(prev)

    @pl.when(jnp.logical_not(has_next))
    def _():
        nxt[...] = jnp.zeros_like(nxt)
        cnext[...] = jnp.zeros_like(cnext)

    for load in loads:
        load.wait()
    pltpu.make_async_copy(seg_ref, seg_ref, seg_sem).wait()

    lane = lax.broadcasted_iota(jnp.int32, (rows, PAIR), 1)
    low = lane < HEAD_DIM

    def only(block, h):
        keep = low if h % 2 == 0 else jnp.logical_not(low)
        return jnp.where(keep, block.astype(F32), 0.0).astype(BF16)

    def cols(g):
        return slice(g * PAIR, (g + 1) * PAIR)

    def head_rows(h):
        return slice(h * HEAD_DIM, (h + 1) * HEAD_DIM)

    for h in range(heads):
        qm[h] = only(q_ref[:, cols(h // 2)], h)
        km[h] = only(kv_ref[h // 2, 0], h)
        vm[h] = only(kv_ref[h // 2, 1], h)

    def seg_row(shard):
        return seg_ref[pl.ds(shard, 1), :]

    def label_col(shard):
        position = lax.broadcasted_iota(jnp.int32, (1, rows), 1)
        label = jnp.where(position < counts_ref[shard], seg_row(shard), -1).astype(F32)
        return jnp.broadcast_to(label, (128, rows)).T

    own_seg = seg_row(s).astype(F32)

    def fill_bias(slot, col, segs, diagonal):
        for part in range(rows // 128):
            at = slice(part * 128, (part + 1) * 128)
            seen = col == segs[:, at]
            if diagonal:
                key_at = lax.broadcasted_iota(jnp.int32, (rows, 128), 0)
                query_at = lax.broadcasted_iota(jnp.int32, (rows, 128), 1) + part * 128
                seen = (seen & (key_at < query_at)) | (key_at == query_at)
            bias[slot, :, at] = jnp.where(seen, 0.0, MASKED)

    colown[...] = label_col(s)
    fill_bias(0, colown[...], own_seg, True)

    def forward_pair(g, kblk, vblk, targets):
        vtr = vblk.astype(F32).T.astype(BF16)
        for slot, masked_q, totals, out, first in targets:
            for h in (2 * g, 2 * g + 1):
                at_top, at_mass = totals(h)
                scores = dot_nt(kblk, masked_q[h]) * to_log2 + bias[slot]
                kept[slot, h] = scores
                top = jnp.max(scores, axis=0, keepdims=True)
                if not first:
                    top = jnp.maximum(at_top[...], top)
                weights = jnp.exp2(scores - top)
                mass = jnp.sum(weights, axis=0, keepdims=True)
                part = dot_nn(vtr[head_rows(h - 2 * g)], weights.astype(BF16))
                if not first:
                    fade = jnp.exp2(at_top[...] - top)
                    mass = mass + at_mass[...] * fade
                    part = part + out[head_rows(h), :] * fade
                at_top[...] = top
                at_mass[...] = mass
                out[head_rows(h), :] = part

    def own_totals(h):
        return stats.at[h:h + 1, :], stats.at[heads + h:heads + h + 1, :]

    def far_totals(h):
        g, at = h // 2, h % 2
        return part_stats.at[g, at:at + 1, :], part_stats.at[g, 2 + at:3 + at, :]

    def own_target(slot, first=False):
        return slot, qm, own_totals, otr, first

    def far_target(slot):
        return slot, qfar, far_totals, ofar, False

    for g in range(pairs):
        forward_pair(g, kv_ref[g, 0], kv_ref[g, 1], [own_target(0, True)])
        part_stats[g, 0:2, :] = jnp.full((2, rows), 2 * MASKED, F32)
        part_stats[g, 2:, :] = jnp.zeros((6, rows), F32)
    ofar[...] = jnp.zeros_like(ofar)

    def own_step(i):
        return jnp.where(odd == 1, i, jnp.where(lax.rem(i, 2) == 1, i + 1, i - 1))

    if near > 2:
        @pl.loop(1, near - 1)
        def _(i):
            j = own_step(i)

            @pl.when(s - j >= 0)
            def _():
                fill_bias(j, label_col(s - j), own_seg, False)

            for g in range(pairs):
                @pl.when(lax.rem(i, 2) == 1)
                def _():
                    kv_up[g].forward(i + 1)

                @pl.when(s - j >= 0)
                def _():
                    @pl.when(lax.rem(j, 2) == 1)
                    def _():
                        kv_up[g].wait(j)

                    forward_pair(g, kvbuf[g, j - 1, 0], kvbuf[g, j - 1, 1], [own_target(j)])

    for d in (near - 1, near):
        @pl.when(s - d >= 0)
        def _():
            col = label_col(s - d)
            fill_bias(d, col, own_seg, False)
            fill_bias(d + 2, col, seg_row(jnp.minimum(s + 2, shards - 1)).astype(F32), False)

    q_down.forward(2, "z")
    for j in range(1, reach + 1):
        @pl.when(s + j < shards)
        def _():
            fill_bias(reach + j, colown[...], seg_row(s + j).astype(F32), False)

    for g in range(pairs):
        @pl.when(helps)
        def _():
            for h in (2 * g, 2 * g + 1):
                qfar[h] = only(qbuf[1, :, cols(g)], h)

        kv_up[g].forward(near)
        j = own_step(near - 1)

        @pl.when(s - j >= 0)
        def _():
                @pl.when(lax.rem(j, 2) == 1)
                def _():
                    kv_up[g].wait(j)

                forward_pair(g, kvbuf[g, j - 1, 0], kvbuf[g, j - 1, 1], [far_target(j + 2), own_target(j)])

        last_j = own_step(near)

        @pl.when(s - last_j >= 0)
        def _():
                @pl.when(lax.rem(last_j, 2) == 1)
                def _():
                    kv_up[g].wait(last_j)

                forward_pair(g, kvbuf[g, last_j - 1, 0], kvbuf[g, last_j - 1, 1], [far_target(last_j + 2)])

        @pl.when(helps)
        def _():
            part_out[g] = ofar[cols(g), :].astype(BF16)
            for copy in far_copies(g):
                copy.start()

        @pl.when(s - last_j >= 0)
        def _():
            forward_pair(g, kvbuf[g, last_j - 1, 0], kvbuf[g, last_j - 1, 1], [own_target(last_j)])

    @pl.when(s + 2 < shards)
    def _():
        for h in range(heads):
            ahead[h] = dot_nt(km[h], qbuf[1, :, cols(h // 2)]) * to_log2 + bias[reach + 2]

    for g in range(pairs):
        @pl.when(helped)
        def _():
            for copy in far_copies(g):
                copy.wait_recv()
            for at in (0, 1):
                h = 2 * g + at
                at_top, at_mass = own_totals(h)
                far_top = far_stats[g, at:at + 1, :]
                top = jnp.maximum(at_top[...], far_top)
                fade, far_fade = jnp.exp2(at_top[...] - top), jnp.exp2(far_top - top)
                at_top[...] = top
                at_mass[...] = at_mass[...] * fade + far_stats[g, 2 + at:3 + at, :] * far_fade
                far_part = far_out[g, head_rows(at), :].astype(F32)
                otr[head_rows(h), :] = otr[head_rows(h), :] * fade + far_part * far_fade

        for h in (2 * g, 2 * g + 1):
            atr[head_rows(h), :] = otr[head_rows(h), :] / stats[heads + h:heads + h + 1, :]
        block = atr[cols(g), :]
        aown[g] = block.T.astype(BF16)
        atr[cols(g), :] = block.astype(BF16).astype(F32)
        pair_copy(1 + g, aown.at[g], aoth.at[g]).start()
    for h in range(heads):
        stats[h:h + 1, :] = stats[h:h + 1, :] + jnp.log(stats[heads + h:heads + h + 1, :]) * LOG2E

    mixed = res_ref[...].astype(F32)
    w_own = w_ref[:, own_cols]
    for g in range(pairs):
        mixed = mixed + dot_nn(aown[g], w_own[cols(g), :])
    w_copy.wait_recv()
    for g in range(pairs):
        pair_copy(1 + g, aown.at[g], aoth.at[g]).wait_recv()
        mixed = mixed + dot_nn(aoth[g], woth[cols(g), :])
    hid[...] = mixed.astype(BF16)

    @pl.when(has_next)
    def _():
        last_copy.start()

    @pl.when(has_prev)
    def _():
        first_copy.start()

    q_down.send(0, "y")
    q_down.send(2, "y")

    @pl.loop(2, reach // 2 + 1)
    def _(i):
        q_down.forward(2 * i)

    long = rows + HALO
    tap_count = taps_ref.shape[0]
    taps = taps_ref[...].astype(F32)

    def shift_hidden(start, stop):
        for r in range(8):
            shifted[r, start:stop, :] = ext[start - r:stop - r, :]

    def shift_grad(start, stop):
        for r in range(8):
            spread[r, start:stop, :] = gconv[start + r:stop + r, :]

    def convolve(g, start, stop):
        size = stop - start
        mix = jnp.zeros((size, PAIR), F32)
        for tap in range(tap_count):
            at = HALO + start - 8 * (tap // 8)
            mix = mix + taps[tap:tap + 1, cols(g)] * shifted[tap % 8, at:at + size, cols(g)]
        gate = jax.nn.sigmoid(mix)
        if start < rows:
            up = cot_ref[start:stop, cols(g)].astype(F32)
            hidden = ext[HALO + start:HALO + stop, cols(g)]
            out_ref[start:stop, cols(g)] = (hidden + mix * gate).astype(BF16)
        else:
            up = cnext[:, cols(g)].astype(F32)
        gconv[start:stop, cols(g)] = up * gate * (1.0 + mix * (1.0 - gate))

    def convolve_back(g, start, stop):
        grad = cot_ref[start:stop, cols(g)].astype(F32)
        for tap in range(tap_count):
            at = start + 8 * (tap // 8)
            grad = grad + taps[tap:tap + 1, cols(g)] * spread[tap % 8, at:at + stop - start, cols(g)]
        gown[g, start:stop, :] = grad.astype(BF16)

    ext[HALO:HALO + rows, :] = hid[...].astype(F32)
    gconv[long:, :] = jnp.zeros((8, width), F32)
    shift_hidden(HALO + 8, HALO + rows)
    step, back_step = (rows - HALO) // 2, (rows - 2 * HALO) // 2
    for g in range(pairs):
        for start in range(HALO, rows, step):
            convolve(g, start, start + step)
    shift_grad(HALO, rows - 8)
    for g in range(pairs):
        for start in range(HALO, rows - HALO, back_step):
            convolve_back(g, start, start + back_step)

    @pl.when(has_next)
    def _():
        first_copy.wait_recv()
        cot_copy.wait_recv()

    @pl.when(has_prev)
    def _():
        last_copy.wait_recv()

    ext[0:HALO, :] = prev[...].astype(F32)
    ext[HALO + rows:, :] = nxt[...].astype(F32)
    shift_hidden(8, HALO + 8)
    shift_hidden(HALO + rows, long + HALO)
    for g in range(pairs):
        convolve(g, 0, HALO)
        convolve(g, rows, long)
    shift_grad(0, HALO)
    shift_grad(rows - 8, long)
    for g in range(pairs):
        convolve_back(g, 0, HALO)
        convolve_back(g, rows - HALO, rows)
        gin_ref[:, cols(g)] = gown[g]
        pair_copy(1 + pairs + g, gown.at[g], goth.at[g]).start()

    w_mine = [w_ref[:, pl.ds(pl.multiple_of(mp * width + g * PAIR, PAIR), PAIR)] for g in range(pairs)]
    w_far = [w_ref[:, pl.ds(pl.multiple_of(other * width + g * PAIR, PAIR), PAIR)] for g in range(pairs)]
    grad = dot_nt(gown[0], w_mine[0])
    gradt = dot_nt(w_mine[0], gown[0])
    for g in range(1, pairs):
        grad = grad + dot_nt(gown[g], w_mine[g])
        gradt = gradt + dot_nt(w_mine[g], gown[g])
    for g in range(pairs):
        pair_copy(1 + pairs + g, gown.at[g], goth.at[g]).wait_recv()
        grad = grad + dot_nt(goth[g], w_far[g])
        gradt = gradt + dot_nt(w_far[g], goth[g])
    for g in range(pairs):
        da[g] = grad[:, cols(g)].astype(BF16)
    products = gradt.astype(BF16).astype(F32) * atr[...]
    for h in range(heads):
        stats[heads + h:heads + h + 1, :] = jnp.sum(products[head_rows(h)], axis=0, keepdims=True)
    s_down.send(0)
    for g in range(pairs):
        a_down[g].send(0)
    for h in range(heads):
        am[h] = only(da[h // 2], h)

    def query_pair(slot, g, kblk, vblk, masked_a, tops, dots, grad_q, first, own=False):
        ktr = kblk.astype(F32).T.astype(BF16)
        sums = []
        for h in (2 * g, 2 * g + 1):
            weights = jnp.exp2(kept[slot, h] - tops(h))
            pushes = dot_nt(vblk, masked_a[h])
            slopes = (weights * (pushes - dots(h))).astype(BF16)
            part = dot_nn(ktr[head_rows(h - 2 * g)], slopes)
            grad_q[head_rows(h), :] = part if first else grad_q[head_rows(h), :] + part
            if own:
                sums.append((dot_nn(slopes, q_ref[:, cols(g)]),
                             dot_nn(weights.astype(BF16), da[g])))
        if own:
            dkacc[:, cols(g)] = jnp.where(low, sums[0][0], sums[1][0])
            dvacc[:, cols(g)] = jnp.where(low, sums[0][1], sums[1][1])

    own_rows = (lambda h: stats[h:h + 1, :], lambda h: stats[heads + h:heads + h + 1, :])
    far_rows = (lambda h: sbuf[1, h:h + 1, :], lambda h: sbuf[1, heads + h:heads + h + 1, :])

    for g in range(pairs):
        query_pair(0, g, kv_ref[g, 0], kv_ref[g, 1], am, *own_rows, dqt, True, True)

    def own_queries(i):
        @pl.when(s - i >= 0)
        def _():
            for g in range(pairs):
                query_pair(i, g, kvbuf[g, i - 1, 0], kvbuf[g, i - 1, 1], am, *own_rows, dqt, False)

    def key_pair(j, g):
        qblk, ablk, far = qbuf[j - 1, :, cols(g)], abuf[g, j - 1], sbuf[j - 1]
        sums = []
        for h in (2 * g, 2 * g + 1):
            if isinstance(j, int) and j == 2:
                scores = ahead[h]
            else:
                scores = dot_nt(km[h], qblk) * to_log2 + bias[reach + j]
            weights = jnp.exp2(scores - far[h:h + 1, :])
            pushes = dot_nt(vm[h], ablk)
            slopes = (weights * (pushes - far[heads + h:heads + h + 1, :])).astype(BF16)
            sums.append((dot_nn(slopes, qblk), dot_nn(weights.astype(BF16), ablk)))
        dkacc[:, cols(g)] = dkacc[:, cols(g)] + jnp.where(low, sums[0][0], sums[1][0])
        dvacc[:, cols(g)] = dvacc[:, cols(g)] + jnp.where(low, sums[0][1], sums[1][1])

    def forward_grad(j):
        s_down.forward(j)
        for g in range(pairs):
            a_down[g].forward(j)

    def keys_even(j):
        @pl.when(s + j < shards)
        def _():
            for g in range(pairs):
                key_pair(j, g)

    def keys_odd(j):
        @pl.when(s + j < shards)
        def _():
            s_down.wait(j)
            q_down.wait(j)
            for g in range(pairs):
                a_down[g].wait(j)
                key_pair(j, g)

    def far_grads(both, parts):
        for g in parts:
            for h in (2 * g, 2 * g + 1):
                afar[h] = only(abuf[g, 1], h)
            for d in (near - 1, near)[:2 if both else 1]:
                query_pair(d + 2, g, kvbuf[g, d - 1, 0], kvbuf[g, d - 1, 1], afar, *far_rows, dfar, d < near)
            part_dq[g] = dfar[cols(g), :].astype(BF16)
            far_grad_copy(g).start()

    if near == 2:
        own_queries(1)
        own_queries(2)
    else:
        pl.loop(1, near + 1)(own_queries)

    def far_step(parity, parts):
        @pl.when(helps & (odd == parity) & (s >= near))
        def _():
            far_grads(True, parts)

        if (near - 1) % 2 == parity:
            @pl.when(helps & (s == near - 1))
            def _():
                far_grads(False, parts)

    forward_grad(2)
    far_step(1, range(pairs))
    keys_even(2)
    keys_odd(1)
    far_step(0, range(1))
    forward_grad(4)
    far_step(0, range(1, pairs))
    keys_even(4)
    def finish_queries():
        @pl.when(helped)
        def _():
            for g in range(pairs):
                far_grad_copy(g).wait_recv()
                dqt[cols(g), :] = dqt[cols(g), :] + far_dq[g].astype(F32)

        gq_ref[...] = (dqt[...] * scale).T.astype(BF16)

    @pl.when(s < reach)
    def _():
        finish_queries()

    keys_odd(3)

    if reach > 4:
        @pl.loop(3, reach // 2 + 1)
        def _(i):
            forward_grad(2 * i)
            keys_even(2 * i)
            keys_odd(2 * i - 1)

    @pl.when(s >= reach)
    def _():
        finish_queries()

    gk_ref[...] = (dkacc[...] * scale).astype(BF16)
    gv_ref[...] = dvacc[...].astype(BF16)

    flat = (*kv_up, q_down, *a_down, s_down)
    for relay in flat:
        relay.finish(0)

    @pl.loop(1, reach // 2 + 1)
    def _(i):
        for relay in flat:
            relay.finish(2 * i)

    @pl.when(helps)
    def _():
        for g in range(pairs):
            for copy in (*far_copies(g), far_grad_copy(g)):
                copy.wait_send()

    w_copy.wait_send()
    for g in range(pairs):
        pair_copy(1 + g, aown.at[g], aoth.at[g]).wait_send()
        pair_copy(1 + pairs + g, gown.at[g], goth.at[g]).wait_send()

    @pl.when(has_prev)
    def _():
        cot_copy.wait_send()
        first_copy.wait_send()

    @pl.when(has_next)
    def _():
        last_copy.wait_send()


def store_kernel(*refs):
    count = len(refs) // 2
    stores = [pltpu.make_async_copy(refs[index], refs[count + index], refs[-1].at[index])
              for index in range(count)]
    for store in stores:
        store.start()
    for store in stores:
        store.wait()


def local(queries, keys, values, residual_in, out_proj, conv_kernel, valid_counts, segment_ids,
          cotangent):
    rows, width = queries.shape
    heads = width // HEAD_DIM
    pairs = width // PAIR
    shards = valid_counts.shape[0]
    window = segment_ids.shape[0]
    reach = -(-(window // 2) // rows)
    block = (rows, width)
    sems = pltpu.SemaphoreType.DMA
    near = reach - 2
    part_rows = (pairs, PAIR, rows)

    def relay_sems(span, parts=()):
        return [sems(parts + (span,)), sems(parts + (span // 2 + 1,)), sems(parts + (span // 2 + 1,))]

    scratch = [pltpu.VMEM(block, BF16), pltpu.VMEM((pairs, 2, rows, PAIR), BF16),
               pltpu.VMEM(block, BF16)] + [
        pltpu.VMEM(out_proj.shape, BF16), pltpu.VMEM(conv_kernel.shape, BF16),
        pltpu.VMEM(block, BF16), pltpu.SMEM(valid_counts.shape, jnp.int32),
        pltpu.VMEM((shards, rows), jnp.int32),
        pltpu.SemaphoreType.DMA((6,)), pltpu.SemaphoreType.DMA((pairs, 2)), pltpu.SemaphoreType.DMA,
        pltpu.VMEM((pairs, near, 2, rows, PAIR), BF16),
        pltpu.VMEM((reach,) + block, BF16), pltpu.VMEM((pairs, reach, rows, PAIR), BF16),
        pltpu.VMEM((reach, 2 * heads, rows), F32),
        pltpu.VMEM(block, BF16),
        pltpu.VMEM((pairs, rows, PAIR), BF16), pltpu.VMEM((pairs, rows, PAIR), BF16),
        pltpu.VMEM((pairs, rows, PAIR), BF16),
        pltpu.VMEM(block, BF16), pltpu.VMEM((HALO, width), BF16), pltpu.VMEM((HALO, width), BF16),
        pltpu.VMEM((HALO, width), BF16),
        pltpu.VMEM((2 * reach + 1, rows, rows), F32), pltpu.VMEM((reach + 1, heads, rows, rows), F32), pltpu.VMEM((rows, 128), F32),
        pltpu.VMEM((heads, rows, PAIR), BF16), pltpu.VMEM((heads, rows, PAIR), BF16),
        pltpu.VMEM((heads, rows, PAIR), BF16), pltpu.VMEM((heads, rows, PAIR), BF16),
        pltpu.VMEM((width, rows), F32), pltpu.VMEM((2 * heads, rows), F32),
        pltpu.VMEM((width, rows), F32), pltpu.VMEM((width, rows), F32),
        pltpu.VMEM(block, F32), pltpu.VMEM(block, F32),
        pltpu.VMEM((pairs, rows, PAIR), BF16), pltpu.VMEM((rows + 2 * HALO, width), F32),
        pltpu.VMEM((8, rows + 2 * HALO, width), F32), pltpu.VMEM((8, rows + HALO, width), F32),
        pltpu.VMEM((rows + HALO + 8, width), F32),
        pltpu.VMEM((pairs, rows, PAIR), BF16),
        pltpu.VMEM((heads, rows, PAIR), BF16), pltpu.VMEM((heads, rows, PAIR), BF16),
        pltpu.VMEM((width, rows), F32), pltpu.VMEM((width, rows), F32),
        pltpu.VMEM(part_rows, BF16), pltpu.VMEM((pairs, 8, rows), F32),
        pltpu.VMEM(part_rows, BF16), pltpu.VMEM((pairs, 8, rows), F32),
        pltpu.VMEM(part_rows, BF16), pltpu.VMEM(part_rows, BF16),
        pltpu.VMEM((heads, rows, rows), F32),
    ] + relay_sems(near, (pairs,)) + relay_sems(reach) + relay_sems(reach, (pairs,)) + relay_sems(reach) + [
        pltpu.SemaphoreType.DMA((1 + 2 * pairs,)), pltpu.SemaphoreType.DMA((1 + 2 * pairs,)),
        pltpu.SemaphoreType.DMA((3,)), pltpu.SemaphoreType.DMA((3,)),
        pltpu.SemaphoreType.DMA((3 * pairs,)), pltpu.SemaphoreType.DMA((3 * pairs,)),
    ]
    vmem = pl.BlockSpec(memory_space=pltpu.VMEM)
    hbm = pl.BlockSpec(memory_space=pltpu.MemorySpace.HBM)
    results = pl.pallas_call(
        functools.partial(kernel, shards, reach, heads),
        out_shape=(pltpu.VMEM(block, BF16),) * 5,
        in_specs=[hbm] * 9,
        out_specs=(vmem,) * 5,
        scratch_shapes=scratch,
        compiler_params=pltpu.CompilerParams(
            collective_id=0, has_side_effects=True, vmem_limit_bytes=VMEM_BYTES),
    )(valid_counts, segment_ids, queries, keys, values, residual_in, out_proj,
      conv_kernel, cotangent)
    return pl.pallas_call(
        store_kernel,
        out_shape=(jax.ShapeDtypeStruct(block, BF16),) * 5,
        in_specs=[pl.BlockSpec(memory_space=pl.ANY)] * 5,
        out_specs=(hbm,) * 5,
        scratch_shapes=[pltpu.SemaphoreType.DMA((5,))],
    )(*[pltpu.with_memory_space_constraint(r, pltpu.VMEM) for r in results])


def solution(mesh):
    tokens = P(("groups", "tm"), "mp")
    in_specs = (tokens, tokens, tokens, tokens, P("mp", None), P(None, "mp"), P("groups"),
                P("groups"), tokens)
    return jax.shard_map(local, mesh=mesh, in_specs=in_specs, out_specs=(tokens,) * 5,
                         check_vma=False)
```
